256 devices in a mesh: gz: 8 (over x, core), ty: 8 (over z), tx: 4 (over y).
Axes of the slice: x: 4, y: 4, z: 8, core: 2. Of those that a mesh axis runs over, the one named last changes fastest.
Arguments:
- images: bfloat16 [8, 4096, 2048], P('gz', 'ty', 'tx'), may hold values from -40 to 40, as said below
- boundary: bfloat16 [4096, 2048], P('ty', 'tx'), may hold values from -40 to 40, as said below
- anchor: float32 [8, 1024, 512], P('gz', 'ty', 'tx'), may hold values from 0.02 to 0.5
Outputs:
- mesh_shift: float32 [8, 2, 1024, 512], P('gz', None, 'ty', 'tx')
- drift: float32 [8, 8, 4, 2, 128], P('gz', 'ty', 'tx')
The draws below stay inside these ranges and needn't reach their ends.
Inputs may be any that keep to these rules, and one draw needn't show every extreme that they name: `images`: pixel intensities. `boundary`: pixel intensities.
All inputs are finite; a program needn't handle non-finite values.
Results may differ from the reference program's by a relative error of at most 0.0003.
Values may be sent and summed in bfloat16 or wider, within the bound.
A program may use at most 64 MiB of HBM per device.

```python
import math
import jax
import jax.numpy as jnp
from jax import lax

PATCH = 128
STRIDE = 4
SWEEPS = 32
TILE = 512
NODES = 128
NZ = 8
NY = 4096
NX = 2048
MY = 1024
MX = 512
N_TY = 8
N_TX = 4


def box_blur(field):
    rows_sum = field
    for lag_index in range(1, 8):
        rows_sum = rows_sum + jnp.roll(field, lag_index, axis=0)
    both_sum = rows_sum
    for lag_index in range(1, 8):
        both_sum = both_sum + jnp.roll(rows_sum, lag_index, axis=1)
    return both_sum * 0.125


def layer_texture(key, layer):
    layer_key = jax.random.fold_in(jax.random.fold_in(key, 23), layer)
    white_noise = jax.random.normal(layer_key, (NY, NX), jnp.float32)
    return box_blur(white_noise)


def expand_patches(values):
    return jnp.repeat(jnp.repeat(values, PATCH, axis=0), PATCH, axis=1)


def volume_views(key, first, count):
    subkeys = jax.random.split(jax.random.fold_in(key, 11), 3)
    grid_rows = NY // PATCH
    grid_cols = NX // PATCH
    segment = jnp.cumsum(jax.random.randint(subkeys[0], (NZ + 1, 2), -3, 4), axis=0).astype(jnp.int32)
    oblique = jax.random.randint(subkeys[1], (NZ + 3, 2, grid_rows, grid_cols), -2, 3).astype(jnp.int32)
    row_index = jnp.arange(NY, dtype=jnp.int32)[:, None]
    col_index = jnp.arange(NX, dtype=jnp.int32)[None, :]

    def section_view(section):
        total = jnp.zeros((NY, NX), jnp.float32)
        moves = lax.dynamic_index_in_dim(segment, section, 0, keepdims=False)
        for depth in (-1, 0, 1):
            layer = section + depth + 1
            texture = layer_texture(key, layer)
            slope = lax.dynamic_index_in_dim(oblique, layer, 0, keepdims=False)
            row_move = moves[0] - depth * expand_patches(slope[0])
            col_move = moves[1] - depth * expand_patches(slope[1])
            source = (row_index - row_move) % NY * NX + (col_index - col_move) % NX
            total = total + jnp.take(texture.reshape(-1), source.reshape(-1)).reshape(NY, NX)
        return total
    shared = lax.map(section_view, first + jnp.arange(count, dtype=jnp.int32))
    noise_key = jax.random.fold_in(subkeys[2], first)
    noise = math.sqrt(0.52) * jax.random.normal(noise_key, (count, NY, NX), jnp.float32)
    values = 0.4 * shared + noise
    return jnp.clip(values, -40.0, 40.0)


def draw_images(key, part):
    return volume_views(key, 1, NZ).astype(jnp.bfloat16)


def draw_boundary(key, part):
    return volume_views(key, 0, 1)[0].astype(jnp.bfloat16)


def levels(key, dims, cuts, smallest, largest):
    def one(dim, blocks):
        draws = jax.random.uniform(jax.random.fold_in(jax.random.fold_in(key, 6), dim), (blocks,), jnp.float32, smallest / len(cuts), largest / len(cuts))
        return jnp.repeat(jnp.exp(draws), dims[dim] // blocks).reshape((-1,) + (1,) * (len(dims) - dim - 1))

    factor_of = one(*cuts[0])
    for cut in cuts[1:]:
        factor_of = factor_of * one(*cut)
    return factor_of


def setup_inputs(seed: int = 0) -> dict:
    arg_keys = jax.random.split(jax.random.key(seed), 4)
    images = draw_images(jax.random.fold_in(arg_keys[3], 71), 0)
    boundary = draw_boundary(jax.random.fold_in(arg_keys[3], 71), 0)
    anchor = jnp.clip(jnp.exp(math.log(0.5) - 3.218876 * jax.random.uniform(arg_keys[2], (NZ, MY, MX), jnp.float32) ** levels(arg_keys[2], (NZ, MY, MX), ((0, 8), (1, 8), (2, 4)), -0.2, 0.2)), 0.02, 0.5)
    return dict(images=images, boundary=boundary, anchor=anchor)


highest = lax.Precision.HIGHEST


def hat_weight(offset):
    return jnp.maximum(0.0, 1.0 - jnp.abs(offset))


def spread_table(nodes, patches):
    node_pos = (jnp.arange(nodes, dtype=jnp.float32) + 0.5) * STRIDE / PATCH - 0.5
    centers = jnp.arange(patches, dtype=jnp.float32)
    weights = hat_weight(node_pos[:, None] - centers[None, :])
    return weights / jnp.sum(weights, axis=1, keepdims=True)


def soft_flow(correlation):
    leading = correlation.shape[:-2]
    scores = (correlation / PATCH).reshape(leading + (PATCH * PATCH,))
    weights = jax.nn.softmax(scores, axis=-1).reshape(leading + (PATCH, PATCH))
    lagged = jnp.arange(PATCH, dtype=jnp.int32)
    signed = jnp.where(lagged < PATCH // 2, lagged, lagged - PATCH).astype(jnp.float32)
    along_rows = jnp.sum(weights * signed[:, None], axis=(-2, -1))
    along_cols = jnp.sum(weights * signed[None, :], axis=(-2, -1))
    return jnp.stack([along_rows, along_cols], axis=-1) / STRIDE


def reference(images, boundary, anchor):
    grid_rows = NY // PATCH
    grid_cols = NX // PATCH
    stacked = jnp.concatenate([boundary[None], images], axis=0)
    pixels = stacked.astype(jnp.float32).reshape(NZ + 1, grid_rows, PATCH, grid_cols, PATCH).transpose(0, 1, 3, 2, 4)
    spectra = jnp.fft.fft2(pixels)
    sections = jnp.arange(NZ, dtype=jnp.int32)

    def flows_at(distance):
        def one_section(section):
            earlier = lax.dynamic_index_in_dim(spectra, jnp.maximum(section + 1 - distance, 0).astype(jnp.int32), 0, keepdims=False)
            current = lax.dynamic_index_in_dim(spectra, (section + 1).astype(jnp.int32), 0, keepdims=False)
            correlation = jnp.fft.ifft2(jnp.conj(earlier) * current).real
            return jnp.where(section + 1 >= distance, soft_flow(correlation), 0.0)
        return lax.map(one_section, sections)

    nearer = flows_at(1)
    farther = flows_at(2)
    before = jnp.concatenate([jnp.zeros_like(nearer[:1]), nearer[:-1]], axis=0)
    position = sections[:, None, None, None]
    patch_target = jnp.where(position <= 1, nearer, 0.5 * (nearer + farther - before))
    per_tile = TILE // PATCH
    table = spread_table(NODES, per_tile)
    tiled = patch_target.reshape(NZ, N_TY, per_tile, N_TX, per_tile, 2)
    target = jnp.einsum('ip,zypxqc,jq->zcyixj', table, tiled, table, precision=highest).reshape(NZ, 2, MY, MX)
    weight = anchor[:, None]

    def sweep(counter, mesh):
        padded = jnp.pad(mesh, ((0, 0), (0, 0), (1, 1), (1, 1)))
        beside_all = padded[:, :, 2:, 1:-1] + padded[:, :, :-2, 1:-1] + padded[:, :, 1:-1, 2:] + padded[:, :, 1:-1, :-2]
        return (beside_all + weight * target) / (4.0 + weight)

    mesh_shift = lax.fori_loop(0, SWEEPS, sweep, target)
    blocks = mesh_shift.reshape(NZ, 2, N_TY, NODES, N_TX, NODES)
    down_rows = jnp.mean(blocks[:, 0], axis=4).transpose(0, 1, 3, 2)
    across = jnp.mean(blocks[:, 1], axis=2)
    profile = jnp.stack([down_rows, across], axis=3)
    ramp = jnp.arange(NODES, dtype=jnp.float32)
    landing = jnp.clip(ramp + profile, 0.0, NODES - 1.0)
    maps = hat_weight(landing[..., None] - ramp)
    start = jnp.broadcast_to(jnp.eye(NODES, dtype=jnp.float32), maps.shape[1:])

    def compose_step(carry, section_maps):
        joined = jnp.einsum('yxcij,yxcjk->yxcik', carry, section_maps, precision=highest)
        placed = jnp.einsum('yxcij,j->yxci', joined, ramp, precision=highest) - ramp
        return joined, placed

    outcome = lax.scan(compose_step, start, maps)
    return mesh_shift, outcome[1]
```

```python
import functools
import math

import jax
import jax.numpy as jnp
import numpy as np
from jax import lax
from jax.experimental import pallas as pl
from jax.experimental.pallas import tpu as pltpu
from jax.sharding import PartitionSpec as P

PATCH = 128
STRIDE = 4
SWEEPS = 32
TILE = 512
NODES = 128
PER = TILE // PATCH
WIDE = NODES + 2 * SWEEPS
GROUPS = WIDE // 8
LANES = 2 * WIDE

f32 = jnp.float32
bf16 = jnp.bfloat16
MESH = pl.DeviceIdType.MESH
AROUND = [(dy, dx) for dy in (-1, 0, 1) for dx in (-1, 0, 1)]


def slot(dy, dx):
    return (dy + 1) * 3 + dx + 1


def pieces(table, count):
    parts = []
    rest = np.asarray(table, np.float64)
    for _ in range(count):
        part = rest.astype(jnp.bfloat16)
        parts.append(part)
        rest = rest - part.astype(np.float64)
    return parts


def spread_table():
    pos = (np.arange(NODES) + 0.5) * STRIDE / PATCH - 0.5
    weights = np.maximum(0.0, 1.0 - np.abs(pos[:, None] - np.arange(PER)[None, :]))
    return weights / weights.sum(axis=1, keepdims=True)


def tables():
    half = PATCH // 2
    n = np.arange(PATCH)
    angle = lambda k: 2.0 * np.pi * (n[:, None] * k[None, :] % PATCH) / PATCH
    low, high = np.arange(half), np.arange(1, half)
    cos_low, sin_high = np.cos(angle(low)), np.sin(angle(high))
    last = np.cos(np.pi * n)[:, None]
    zero = np.zeros_like(last)
    basis = np.concatenate([cos_low, last, sin_high], axis=1)
    same = np.concatenate([cos_low, last, cos_low[:, 1:]], axis=1)
    cross = np.concatenate([zero, sin_high, zero, -sin_high], axis=1)
    weight = np.full(PATCH, 2.0 / PATCH)
    weight[[0, half]] = 1.0 / PATCH
    inverse = basis * weight[None, :]

    b_hi, b_lo = pieces(basis, 2)
    s_hi, s_lo = pieces(same, 2)
    c_hi, c_lo = pieces(cross, 2)
    r_hi, r_lo = pieces(inverse.T, 2)
    l_hi, l_lo = pieces(inverse * (math.log2(math.e) / PATCH), 2)
    left = np.concatenate([b_hi.T, b_lo.T], axis=0)
    right = np.concatenate([b_hi, b_lo], axis=1)
    right_pair = np.concatenate([s_hi, c_hi, s_lo, c_lo], axis=1)
    back_right = np.concatenate([r_hi, r_lo], axis=1)
    back_left = np.concatenate([l_hi, l_lo], axis=0)
    twice = lambda t, axis: np.concatenate([t, t], axis=axis)

    spread = spread_table()
    spread_lanes = np.repeat(spread.T, PER, axis=0).astype(np.float32)
    rows = np.zeros((WIDE, 128))
    for group in range(GROUPS):
        for sub in range(8):
            i = sub * GROUPS + group - SWEEPS
            dy = i // NODES
            for piece in range(3):
                first = piece * 32 + (dy + 1) * 8
                rows[group * 8 + sub, first : first + PER] = spread[i - dy * NODES]
    return (
        left,
        twice(right, 0),
        twice(right_pair, 0),
        twice(back_right, 0),
        twice(back_left, 1),
        spread_lanes,
        rows.astype(jnp.bfloat16),
    )


def mm(a, b):
    return jnp.dot(a, b, preferred_element_type=f32)


def halves(value):
    hi = value.astype(bf16)
    return hi, (value - hi.astype(f32)).astype(bf16)


def iota(shape, dim):
    return lax.broadcasted_iota(jnp.int32, shape, dim)


def stacked_rows(wide):
    return jnp.concatenate([wide[:, q * PATCH : (q + 1) * PATCH] for q in range(PER)], axis=0)


def side_by_side(tall):
    return jnp.concatenate([tall[q * PATCH : (q + 1) * PATCH] for q in range(PER)], axis=1)


def row_pass(pixels, left):
    both = mm(left[...], pixels)
    return jnp.concatenate(halves(stacked_rows(both[:PATCH] + both[PATCH:])), axis=1)


def packed_spectrum(pixels, left, right):
    both = mm(row_pass(pixels, left), right[...])
    return both[:, :PATCH] + both[:, PATCH:]


def paired_spectrum(pixels, left, right_pair):
    both = mm(row_pass(pixels, left), right_pair[...])
    return (
        both[:, :PATCH] + both[:, 2 * PATCH : 3 * PATCH],
        both[:, PATCH : 2 * PATCH] + both[:, 3 * PATCH :],
    )


def cross_spectrum(pair, later):
    half = PATCH // 2
    same, cross = pair
    turned = pltpu.roll(later, half, 1)
    first = iota((half, PATCH), 0) == 0
    out = []
    for q in range(PER):
        top = slice(q * PATCH, q * PATCH + half)
        low = slice(q * PATCH + half, (q + 1) * PATCH)
        joint = lambda e, c: same[e] * later[c] + cross[e] * turned[c]
        low_low = joint(low, low)
        out.append(joint(top, top) + jnp.where(first, 0.0, low_low))
        out.append(jnp.where(first, low_low, joint(top, low) - joint(low, top)))
    return jnp.concatenate(out, axis=0)


def scores(product, back_right, back_left):
    both = mm(jnp.concatenate(halves(product), axis=1), back_right[...])
    wide = side_by_side(both[:, :PATCH] + both[:, PATCH:])
    both = mm(back_left[...], jnp.concatenate(halves(wide), axis=0))
    return both[:PATCH] + both[PATCH:]


def signed_lag(shape, dim):
    lag = iota(shape, dim)
    return jnp.where(lag < PATCH // 2, lag, lag - PATCH).astype(f32)


def hat(offset):
    return jnp.maximum(0.0, 1.0 - jnp.abs(offset))


def widen(left, here, right, lane):
    turn = lambda v: pltpu.roll(v, 64, 1)
    centre = turn(here[1])
    return (
        here[0],
        jnp.where(lane < 32, right[0], jnp.where(lane < 64, turn(left[1]), centre)),
        jnp.where(lane < 64, centre, jnp.where(lane < 96, turn(right[1]), left[0])),
    )


def kernel(
    sizes,
    images, boundary, anchor, left, right, right_pair, back_right, back_left, spread_lanes, spread_rows,
    mesh_out, drift_out,
    own, before, after, anchors, patch_in, patch_out, sums, land_in, land_out,
    rate_rows, pull_rows, rate, pull, mesh_a, mesh_b, natural,
    own_sem, before_sem, after_sem, up_sem, down_sem, anchor_sem, anchor_sent, anchor_own,
    patch_sem, patch_sent, land_sem, land_sent,
):
    n_gz, n_ty, n_tx = sizes
    g, y, x = lax.axis_index("gz"), lax.axis_index("ty"), lax.axis_index("tx")

    def inside(dy, dx):
        ok = None
        for pos, step, count in ((y, dy, n_ty), (x, dx, n_tx)):
            if step:
                here = (pos + step >= 0) & (pos + step < count)
                ok = here if ok is None else ok & here
        return (g >= 0) if ok is None else ok

    def band(ref, r):
        return ref.at[pl.ds(pl.multiple_of(r * PATCH, PATCH), PATCH), :]

    for r in range(PER):
        pltpu.make_async_copy(band(images.at[0], r), own.at[r], own_sem.at[r]).start()

        @pl.when(g == 0)
        def _():
            pltpu.make_async_copy(band(boundary, r), before.at[r], before_sem.at[r]).start()

        @pl.when(g == n_gz - 1)
        def _():
            pltpu.make_async_copy(band(boundary, r), after.at[r], after_sem.at[r]).start()

    pltpu.make_async_copy(anchor.at[0], anchors.at[slot(0, 0)], anchor_own).start()

    barrier = pltpu.get_barrier_semaphore()
    greeted = jnp.int32(0)

    def greet(ok, device):
        @pl.when(ok)
        def _():
            pl.semaphore_signal(barrier, inc=1, device_id=device, device_id_type=MESH)

        return jnp.where(ok, 1, 0).astype(jnp.int32)

    for dz in (-1, 1, 0):
        for dy, dx in AROUND:
            if (dz, dy, dx) != (0, 0, 0):
                ok = inside(dy, dx) & (g + dz >= 0) & (g + dz < n_gz)
                greeted += greet(ok, (g + dz, y + dy, x + dx))
    for step in range(2, n_gz):
        greeted += greet(g + step < n_gz, (g + step, y, x))
        greeted += greet(g - step >= 0, (g - step, y, x))

    ramp_rows = iota((16, NODES), 1).astype(f32)
    for t in range(n_gz):

        @pl.when(t >= g)
        def _():
            land_in[t] = ramp_rows

    for dy, dx in AROUND:
        if (dy, dx) != (0, 0):

            @pl.when(jnp.logical_not(inside(dy, dx)))
            def _():
                anchors[slot(dy, dx)] = jnp.zeros((NODES, NODES), f32)
                patch_in[slot(dy, dx)] = jnp.zeros((8, NODES), f32)

        @pl.when(jnp.logical_not(inside(dy, dx)) | (g < 2))
        def _():
            patch_in[9 + slot(dy, dx)] = jnp.zeros((8, NODES), f32)

    pl.semaphore_wait(barrier, greeted)

    def remote(src, dst, sent, arrived, device):
        return pltpu.make_async_remote_copy(
            src_ref=src, dst_ref=dst, send_sem=sent, recv_sem=arrived, device_id=device, device_id_type=MESH
        )

    def to_later(r):
        return remote(band(images.at[0], r), before.at[r], up_sem.at[r], before_sem.at[r], (g + 1, y, x))

    def to_earlier(r):
        return remote(band(images.at[0], r), after.at[r], down_sem.at[r], after_sem.at[r], (g - 1, y, x))

    for r in range(PER):

        @pl.when(g < n_gz - 1)
        def _():
            to_later(r).start()

        @pl.when(g > 0)
        def _():
            to_earlier(r).start()

    rows_of = {-1: (0, SWEEPS), 0: (0, NODES), 1: (NODES - SWEEPS, SWEEPS)}

    def anchor_copy(dy, dx):
        first, count = rows_of[dy]
        to = slot(-dy, -dx)
        return remote(
            anchor.at[0, pl.ds(first, count), :],
            anchors.at[to, pl.ds(first, count), :],
            anchor_sent.at[to],
            anchor_sem.at[to],
            (g, y + dy, x + dx),
        )

    for dy, dx in AROUND:
        if (dy, dx) != (0, 0):

            @pl.when(inside(dy, dx))
            def _():
                anchor_copy(dy, dx).start()

    def arrival(ref, sem):
        pltpu.make_async_copy(ref, ref, sem).wait()

    lag_rows = signed_lag((PATCH, PATCH), 0)

    def softmax_sums(wide, pair, r):
        for q in range(PER):
            score = wide[:, q * PATCH : (q + 1) * PATCH]
            weight = jnp.exp2(score - jnp.max(score))
            at = pl.ds(q * PER + r, 1)
            sums[pair, 0, at, :] = jnp.sum(weight, axis=0, keepdims=True)
            sums[pair, 1, at, :] = jnp.sum(weight * lag_rows, axis=0, keepdims=True)

    def band_step(r, carry):
        arrival(own.at[r], own_sem.at[r])
        here = packed_spectrum(own[r], left, right)
        arrival(before.at[r], before_sem.at[r])
        pair = paired_spectrum(before[r], left, right_pair)
        softmax_sums(scores(cross_spectrum(pair, here), back_right, back_left), 0, r)
        arrival(after.at[r], after_sem.at[r])
        there = packed_spectrum(after[r], left, right)
        softmax_sums(scores(cross_spectrum(pair, there), back_right, back_left), 1, r)
        return carry

    lax.fori_loop(0, PER, band_step, 0)

    lag_lanes = signed_lag((PER * PER, PATCH), 1)
    sub8 = iota((8, NODES), 0)

    def flow(pair):
        weight = sums[pair, 0]
        scale = (1.0 / STRIDE) / jnp.sum(weight, axis=1, keepdims=True)
        rows = jnp.sum(sums[pair, 1], axis=1, keepdims=True) * scale
        cols = jnp.sum(weight * lag_lanes, axis=1, keepdims=True) * scale
        return rows, cols

    def spread_tile(rows, cols):
        def over_cols(value):
            part = value * spread_lanes[...]
            part = part[:8] + part[8:]
            return part + pltpu.roll(part, 4, 0)

        return jnp.where(sub8 < 4, over_cols(rows), over_cols(cols))

    near, far = flow(0), flow(1)
    near_scale = jnp.where(g >= 2, 0.5, 1.0).astype(f32)
    mine = spread_tile(*(near_scale * v for v in near))
    patch_in[slot(0, 0)] = mine
    patch_out[0] = mine
    patch_out[1] = spread_tile(*(0.5 * (b - a) for a, b in zip(near, far)))

    def patch_copy(kind, dy, dx):
        to = 9 * kind + slot(-dy, -dx)
        return remote(
            patch_out.at[kind], patch_in.at[to], patch_sent.at[to], patch_sem.at[to], (g + kind, y + dy, x + dx)
        )

    ahead = (g >= 1) & (g < n_gz - 1)
    for dy, dx in AROUND:

        @pl.when(inside(dy, dx) & ahead)
        def _():
            patch_copy(1, dy, dx).start()

        if (dy, dx) != (0, 0):

            @pl.when(inside(dy, dx))
            def _():
                patch_copy(0, dy, dx).start()

    arrival(anchors.at[slot(0, 0)], anchor_own)
    for dy, dx in AROUND:
        if (dy, dx) != (0, 0):
            first, count = rows_of[-dy]
            part = anchors.at[slot(dy, dx), pl.ds(first, count), :]

            @pl.when(inside(dy, dx))
            def _():
                arrival(part, anchor_sem.at[slot(dy, dx)])

    top = 0
    for dy in (-1, 0, 1):
        first, count = rows_of[-dy]
        lane = iota((count, NODES), 1)
        rates, pulls = [], []
        for dx in (-1, 0, 1):
            tie = anchors[slot(dy, dx), pl.ds(first, count), :]
            held = 1.0 / (4.0 + tie)
            if (dy, dx) != (0, 0):
                held = held * jnp.where(inside(dy, dx), 1.0, 0.0).astype(f32)
            rates.append((held, held))
            pulls.append((tie * held,) * 2)
        for ref, parts in ((rate_rows, rates), (pull_rows, pulls)):
            for block, value in enumerate(widen(*parts, lane)):
                ref[block, top : top + count, :] = value
        top += count
    for group in range(GROUPS):
        for ref, rows in ((rate, rate_rows), (pull, pull_rows)):
            for block in range(3):
                ref[group, :, block * 128 : (block + 1) * 128] = rows[block, pl.ds(group, 8, stride=GROUPS), :]

    for dy, dx in AROUND:

        @pl.when(inside(dy, dx) & (g >= 2))
        def _():
            arrival(patch_in.at[9 + slot(dy, dx)], patch_sem.at[9 + slot(dy, dx)])

        if (dy, dx) != (0, 0):

            @pl.when(inside(dy, dx))
            def _():
                arrival(patch_in.at[slot(dy, dx)], patch_sem.at[slot(dy, dx)])

    lane8 = iota((8, NODES), 1)
    bands = []
    for dy in (-1, 0, 1):
        parts = []
        for dx in (-1, 0, 1):
            tile = patch_in[slot(dy, dx)] + patch_in[9 + slot(dy, dx)]
            parts.append((tile, pltpu.roll(tile, 4, 0)))
        bands.append(jnp.concatenate(widen(*parts, lane8), axis=1))
    bands.append(jnp.zeros((8, LANES), f32))
    patch_rows = jnp.concatenate(bands, axis=0)
    high = patch_rows.astype(bf16)
    rest = patch_rows - high.astype(f32)
    middle = rest.astype(bf16)
    low = (rest - middle.astype(f32)).astype(bf16)
    target = mm(spread_rows[...], jnp.concatenate([high, middle, low, jnp.zeros_like(low)], axis=0))
    for group in range(GROUPS):
        value = target[group * 8 : (group + 1) * 8]
        mesh_a[group] = value
        pull[group] = pull[group] * value

    def sweep(src, dst):
        for group in range(GROUPS):
            here = src[group]
            above = pltpu.roll(src[GROUPS - 1], 1, 0) if group == 0 else src[group - 1]
            below = pltpu.roll(src[0], 7, 0) if group == GROUPS - 1 else src[group + 1]
            beside = pltpu.roll(here, 1, 1) + pltpu.roll(here, LANES - 1, 1)
            dst[group] = ((above + below) + beside) * rate[group] + pull[group]

    def two_sweeps(_, carry):
        sweep(mesh_a, mesh_b)
        sweep(mesh_b, mesh_a)
        return carry

    lax.fori_loop(0, SWEEPS // 2, two_sweeps, 0)

    for group in range(GROUPS):
        value = mesh_a[group]
        turned = [pltpu.roll(value[:, b * 128 : (b + 1) * 128], 64, 1) for b in (1, 2)]
        at = pl.ds(group, 8, stride=GROUPS)
        natural[0, at, :] = value[:, :128]
        natural[1, at, :] = jnp.where(lane8 < 64, turned[0], turned[1])
    rows = natural[0, SWEEPS : SWEEPS + NODES, :]
    cols = natural[1, SWEEPS : SWEEPS + NODES, :]
    mesh_out[0, 0] = rows
    mesh_out[0, 1] = cols

    sub_i, lane_i = iota((NODES, NODES), 0), iota((NODES, NODES), 1)
    sub_f, lane_f = sub_i.astype(f32), lane_i.astype(f32)
    eye = sub_i == lane_i
    to_row = lambda col: jnp.sum(jnp.where(eye, col, 0.0), axis=0, keepdims=True)
    to_col = lambda row: jnp.sum(jnp.where(eye, row, 0.0), axis=1, keepdims=True)
    land = lambda at: jnp.clip(at, 0.0, NODES - 1.0)
    col_0 = land(sub_f[:, :1] + jnp.sum(rows, axis=1, keepdims=True) / NODES)
    row_1 = land(lane_f[:1] + jnp.sum(cols, axis=0, keepdims=True) / NODES)
    row_0 = to_row(col_0)
    sub16 = iota((16, NODES), 0)
    land_out[...] = jnp.where(sub16 == 0, row_0, jnp.where(sub16 == 1, row_1, 0.0))

    def land_copy(step):
        return remote(
            land_out, land_in.at[g], land_sent.at[step - 1], land_sem.at[g], (g + step, y, x)
        )

    for step in range(1, n_gz):

        @pl.when(g + step < n_gz)
        def _():
            land_copy(step).start()

    col_1 = to_col(row_1)
    for t in range(n_gz - 1):

        @pl.when(t < g)
        def _():
            arrival(land_in.at[t], land_sem.at[t])

    for c, column in ((0, col_0), (1, col_1)):
        value = column
        for t in range(n_gz - 2, -1, -1):
            place = land_in[t, c : c + 1, :]
            if (n_gz - 2 - t) % 2 == 0:
                value = jnp.sum(hat(place - sub_f) * value, axis=0, keepdims=True)
            else:
                value = jnp.sum(hat(to_col(place) - lane_f) * value, axis=1, keepdims=True)
        if n_gz % 2:
            value = to_row(value)
        drift_out[0, 0, 0, c : c + 1, :] = value - lane_f[:1]

    for r in range(PER):

        @pl.when(g < n_gz - 1)
        def _():
            to_later(r).wait_send()

        @pl.when(g > 0)
        def _():
            to_earlier(r).wait_send()

    for dy, dx in AROUND:
        if (dy, dx) != (0, 0):

            @pl.when(inside(dy, dx))
            def _():
                anchor_copy(dy, dx).wait_send()
                patch_copy(0, dy, dx).wait_send()

        @pl.when(inside(dy, dx) & ahead)
        def _():
            patch_copy(1, dy, dx).wait_send()

    for step in range(1, n_gz):

        @pl.when(g + step < n_gz)
        def _():
            land_copy(step).wait_send()


def solution(mesh):
    sizes = tuple(mesh.shape[name] for name in ("gz", "ty", "tx"))
    n_gz = sizes[0]
    constants = tables()
    dma = pltpu.SemaphoreType.DMA

    def local(images, boundary, anchor):
        vmem = pl.BlockSpec(memory_space=pltpu.VMEM)
        hbm = pl.BlockSpec(memory_space=pl.ANY)
        return pl.pallas_call(
            functools.partial(kernel, sizes),
            out_shape=(
                jax.ShapeDtypeStruct((1, 2, NODES, NODES), f32),
                jax.ShapeDtypeStruct((1, 1, 1, 2, NODES), f32),
            ),
            in_specs=[hbm] * 3 + [vmem] * len(constants),
            out_specs=(vmem, vmem),
            scratch_shapes=[
                pltpu.VMEM((PER, PATCH, TILE), bf16),
                pltpu.VMEM((PER, PATCH, TILE), bf16),
                pltpu.VMEM((PER, PATCH, TILE), bf16),
                pltpu.VMEM((9, NODES, NODES), f32),
                pltpu.VMEM((18, 8, NODES), f32),
                pltpu.VMEM((2, 8, NODES), f32),
                pltpu.VMEM((2, 2, PER * PER, PATCH), f32),
                pltpu.VMEM((n_gz, 16, NODES), f32),
                pltpu.VMEM((16, NODES), f32),
                pltpu.VMEM((3, WIDE, 128), f32),
                pltpu.VMEM((3, WIDE, 128), f32),
                pltpu.VMEM((GROUPS, 8, LANES), f32),
                pltpu.VMEM((GROUPS, 8, LANES), f32),
                pltpu.VMEM((GROUPS, 8, LANES), f32),
                pltpu.VMEM((GROUPS, 8, LANES), f32),
                pltpu.VMEM((2, WIDE, NODES), f32),
                dma((PER,)),
                dma((PER,)),
                dma((PER,)),
                dma((PER,)),
                dma((PER,)),
                dma((9,)),
                dma((9,)),
                dma,
                dma((18,)),
                dma((18,)),
                dma((n_gz,)),
                dma((n_gz,)),
            ],
            compiler_params=pltpu.CompilerParams(
                collective_id=0, has_side_effects=True, vmem_limit_bytes=48 * 1024 * 1024
            ),
            name="align",
        )(images, boundary, anchor, *(jnp.asarray(c) for c in constants))

    return jax.shard_map(
        local,
        mesh=mesh,
        in_specs=(P("gz", "ty", "tx"), P("ty", "tx"), P("gz", "ty", "tx")),
        out_specs=(P("gz", None, "ty", "tx"), P("gz", "ty", "tx", None, None)),
        check_vma=False,
    )
```

```python
import functools
import math

import jax
import jax.numpy as jnp
import numpy as np
from jax import lax
from jax.experimental import pallas as pl
from jax.experimental.pallas import tpu as pltpu
from jax.sharding import PartitionSpec as P

PATCH = 128
STRIDE = 4
SWEEPS = 32
TILE = 512
NODES = 128
PER = TILE // PATCH
WIDE = NODES + 2 * SWEEPS
GROUPS = WIDE // 8
LANES = 2 * WIDE

GRANT = 48 * 1024 * 1024

f32 = jnp.float32
bf16 = jnp.bfloat16
MESH = pl.DeviceIdType.MESH
AROUND = [(dy, dx) for dy in (-1, 0, 1) for dx in (-1, 0, 1)]


def slot(dy, dx):
    return (dy + 1) * 3 + dx + 1


def pieces(table, count):
    parts = []
    rest = np.asarray(table, np.float64)
    for _ in range(count):
        part = rest.astype(jnp.bfloat16)
        parts.append(part)
        rest = rest - part.astype(np.float64)
    return parts


def spread_table():
    pos = (np.arange(NODES) + 0.5) * STRIDE / PATCH - 0.5
    weights = np.maximum(0.0, 1.0 - np.abs(pos[:, None] - np.arange(PER)[None, :]))
    return weights / weights.sum(axis=1, keepdims=True)


def tables():
    half = PATCH // 2
    n = np.arange(PATCH)
    angle = lambda k: 2.0 * np.pi * (n[:, None] * k[None, :] % PATCH) / PATCH
    low, high = np.arange(half), np.arange(1, half)
    cos_low, sin_high = np.cos(angle(low)), np.sin(angle(high))
    last = np.cos(np.pi * n)[:, None]
    zero = np.zeros_like(last)
    basis = np.concatenate([cos_low, last, sin_high], axis=1)
    same = np.concatenate([cos_low, last, cos_low[:, 1:]], axis=1)
    cross = np.concatenate([zero, sin_high, zero, -sin_high], axis=1)
    weight = np.full(PATCH, 2.0 / PATCH)
    weight[[0, half]] = 1.0 / PATCH
    inverse = basis * weight[None, :]

    b_hi, b_lo = pieces(basis, 2)
    s_hi, s_lo = pieces(same, 2)
    c_hi, c_lo = pieces(cross, 2)
    r_hi, r_lo = pieces(inverse.T, 2)
    l_hi, l_lo = pieces(inverse * (math.log2(math.e) / PATCH), 2)
    left = np.concatenate([b_hi.T, b_lo.T], axis=0)
    right = np.concatenate([b_hi, b_lo], axis=1)
    right_pair = np.concatenate([s_hi, c_hi, s_lo, c_lo], axis=1)
    back_right = np.concatenate([r_hi, r_lo], axis=1)
    back_left = np.concatenate([l_hi, l_lo], axis=0)
    twice = lambda t, axis: np.concatenate([t, t], axis=axis)

    spread = spread_table()
    rows = np.zeros((WIDE, 128))
    for group in range(GROUPS):
        for sub in range(8):
            i = sub * GROUPS + group - SWEEPS
            dy = i // NODES
            for piece in range(3):
                first = piece * 32 + (dy + 1) * 8
                rows[group * 8 + sub, first : first + PER] = spread[i - dy * NODES]
    cols = np.zeros((128, LANES))
    take = np.zeros((256, LANES))
    give = np.zeros((LANES, 2 * NODES))
    for u in range(3):
        for lane in range(128):
            comp, j = lane // 64, lane % 64 * 3 + u - SWEEPS
            dx = j // NODES
            at = u * 128 + lane
            for piece in range(3):
                first = piece * 32 + (dx + 1) * 8 + comp * PER
                cols[first : first + PER, at] = spread[j - dx * NODES]
            take[j if dx == 0 else 128 + j % NODES, at] = 1.0
            if dx == 0:
                give[at, comp * NODES + j] = 1.0
    return tuple(
        t.astype(jnp.bfloat16)
        for t in (
            left,
            twice(right, 0),
            twice(right_pair, 0),
            twice(back_right, 0),
            twice(back_left, 1),
            take,
            cols,
            rows,
            give,
        )
    )


def mm(a, b):
    return jnp.dot(a, b, preferred_element_type=f32)


def halves(value):
    hi = value.astype(bf16)
    return hi, (value - hi.astype(f32)).astype(bf16)


def iota(shape, dim):
    return lax.broadcasted_iota(jnp.int32, shape, dim)


def stacked_rows(wide):
    return jnp.concatenate([wide[:, q * PATCH : (q + 1) * PATCH] for q in range(PER)], axis=0)


def side_by_side(tall):
    return jnp.concatenate([tall[q * PATCH : (q + 1) * PATCH] for q in range(PER)], axis=1)


def row_pass(pixels, left):
    both = mm(left[...], pixels)
    return jnp.concatenate(halves(stacked_rows(both[:PATCH] + both[PATCH:])), axis=1)


def packed_spectrum(pixels, left, right):
    both = mm(row_pass(pixels, left), right[...])
    return both[:, :PATCH] + both[:, PATCH:]


def paired_spectrum(pixels, left, right_pair):
    both = mm(row_pass(pixels, left), right_pair[...])
    return (
        both[:, :PATCH] + both[:, 2 * PATCH : 3 * PATCH],
        both[:, PATCH : 2 * PATCH] + both[:, 3 * PATCH :],
    )


def cross_spectrum(pair, later):
    half = PATCH // 2
    same, cross = pair
    turned = pltpu.roll(later, half, 1)
    first = iota((half, PATCH), 0) == 0
    out = []
    for q in range(PER):
        top = slice(q * PATCH, q * PATCH + half)
        low = slice(q * PATCH + half, (q + 1) * PATCH)
        joint = lambda e, c: same[e] * later[c] + cross[e] * turned[c]
        low_low = joint(low, low)
        out.append(joint(top, top) + jnp.where(first, 0.0, low_low))
        out.append(jnp.where(first, low_low, joint(top, low) - joint(low, top)))
    return jnp.concatenate(out, axis=0)


def scores(product, back_right, back_left):
    both = mm(jnp.concatenate(halves(product), axis=1), back_right[...])
    wide = side_by_side(both[:, :PATCH] + both[:, PATCH:])
    both = mm(back_left[...], jnp.concatenate(halves(wide), axis=0))
    return both[:PATCH] + both[PATCH:]


def signed_lag(shape, dim):
    lag = iota(shape, dim)
    return jnp.where(lag < PATCH // 2, lag, lag - PATCH).astype(f32)


def hat(offset):
    return jnp.maximum(0.0, 1.0 - jnp.abs(offset))


def thirds(value):
    high = value.astype(bf16)
    rest = value - high.astype(f32)
    middle = rest.astype(bf16)
    return high, middle, (rest - middle.astype(f32)).astype(bf16)


def moved(value, selection):
    count = value.shape[0]
    parts = mm(jnp.concatenate(thirds(value), axis=0), selection)
    return parts[:count] + parts[count : 2 * count] + parts[2 * count :]


def kernel(
    sizes,
    images, boundary, anchor, *rest,
):
    n_gz, n_ty, n_tx = sizes
    tables_in, rest = rest[:9], rest[9:]
    (
        mesh_out, land_all,
        own, before, after, spectra, ties, patch_in, patch_out, sums, land_in, land_out,
        rate, pull, mesh_a, mesh_b,
    ) = rest[:16]
    tables_here, rest = rest[16:25], rest[25:]
    (
        table_sem, own_sem, before_sem, after_sem, up_sem, down_sem, tie_sem, tie_sent,
        patch_sem, patch_sent, land_sem, land_sent,
    ) = rest
    left, right, right_pair, back_right, back_left, take, spread_cols, spread_rows, give = tables_here
    g, y, x = lax.axis_index("gz"), lax.axis_index("ty"), lax.axis_index("tx")

    def inside(dy, dx):
        ok = None
        for pos, step, count in ((y, dy, n_ty), (x, dx, n_tx)):
            if step:
                here = (pos + step >= 0) & (pos + step < count)
                ok = here if ok is None else ok & here
        return (g >= 0) if ok is None else ok

    barrier = pltpu.get_barrier_semaphore()
    greeted = jnp.int32(0)

    def greet(ok, device):
        @pl.when(ok)
        def _():
            pl.semaphore_signal(barrier, inc=1, device_id=device, device_id_type=MESH)

        return jnp.where(ok, 1, 0).astype(jnp.int32)

    for step in range(2, n_gz):
        greeted += greet(g + step < n_gz, (g + step, y, x))
        greeted += greet(g - step >= 0, (g - step, y, x))
    for dz in (-1, 1, 0):
        for dy, dx in AROUND:
            if (dz, dy, dx) != (0, 0, 0):
                ok = inside(dy, dx) & (g + dz >= 0) & (g + dz < n_gz)
                greeted += greet(ok, (g + dz, y + dy, x + dx))

    def band(ref, r):
        return ref.at[pl.ds(pl.multiple_of(r * PATCH, PATCH), PATCH), :]

    table_copies = [
        pltpu.make_async_copy(src, dst, table_sem.at[i])
        for i, (src, dst) in enumerate(zip(tables_in, tables_here))
    ]
    for copy in table_copies[:2]:
        copy.start()
    for r in range(PER):
        pltpu.make_async_copy(band(images.at[0], r), own.at[r], own_sem.at[r]).start()
    for copy in table_copies[2:]:
        copy.start()
    tie_own = pltpu.make_async_copy(
        anchor.at[0], ties.at[1, pl.ds(SWEEPS, NODES), :], tie_sem.at[slot(0, 0)]
    )
    tie_own.start()
    for r in range(PER):

        @pl.when(g == 0)
        def _():
            pltpu.make_async_copy(band(boundary, r), before.at[r], before_sem.at[r]).start()

        @pl.when(g == n_gz - 1)
        def _():
            pltpu.make_async_copy(band(boundary, r), after.at[r], after_sem.at[r]).start()

    ramp_rows = iota((8, NODES), 1).astype(f32)
    for t in range(n_gz):

        @pl.when(t >= g)
        def _():
            land_in[t] = ramp_rows

    for edge, count, first in ((y == 0, SWEEPS, 0), (y == n_ty - 1, SWEEPS, SWEEPS + NODES)):

        @pl.when(edge)
        def _():
            for d in range(3):
                ties[d, pl.ds(first, count), :] = jnp.zeros((count, NODES), f32)

    for edge, d in ((x == 0, 0), (x == n_tx - 1, 2)):

        @pl.when(edge)
        def _():
            ties[d] = jnp.zeros((WIDE, NODES), f32)

    for dy, dx in AROUND:
        if (dy, dx) != (0, 0):

            @pl.when(jnp.logical_not(inside(dy, dx)))
            def _():
                patch_in[slot(dy, dx)] = jnp.zeros((8, NODES), f32)

        @pl.when(jnp.logical_not(inside(dy, dx)) | (g < 2))
        def _():
            patch_in[9 + slot(dy, dx)] = jnp.zeros((8, NODES), f32)

    pl.semaphore_wait(barrier, greeted)

    def remote(src, dst, sent, arrived, device):
        return pltpu.make_async_remote_copy(
            src_ref=src, dst_ref=dst, send_sem=sent, recv_sem=arrived, device_id=device, device_id_type=MESH
        )

    def to_later(r):
        return remote(band(images.at[0], r), before.at[r], up_sem.at[r], before_sem.at[r], (g + 1, y, x))

    def to_earlier(r):
        return remote(band(images.at[0], r), after.at[r], down_sem.at[r], after_sem.at[r], (g - 1, y, x))

    for r in range(PER):

        @pl.when(g < n_gz - 1)
        def _():
            to_later(r).start()

        @pl.when(g > 0)
        def _():
            to_earlier(r).start()

    rows_of = {-1: (0, SWEEPS), 0: (0, NODES), 1: (NODES - SWEEPS, SWEEPS)}
    place_of = {-1: 0, 0: SWEEPS, 1: SWEEPS + NODES}

    def tie_copy(dy, dx):
        first, count = rows_of[dy]
        to = slot(-dy, -dx)
        return remote(
            anchor.at[0, pl.ds(first, count), :],
            ties.at[1 - dx, pl.ds(place_of[-dy], count), :],
            tie_sent.at[to],
            tie_sem.at[to],
            (g, y + dy, x + dx),
        )

    for dy, dx in AROUND:
        if (dy, dx) != (0, 0):

            @pl.when(inside(dy, dx))
            def _():
                tie_copy(dy, dx).start()

    def arrival(ref, sem):
        pltpu.make_async_copy(ref, ref, sem).wait()

    for copy in table_copies[:2]:
        copy.wait()

    def own_step(r, carry):
        arrival(own.at[r], own_sem.at[r])
        spectra[r] = packed_spectrum(own[r], left, right)
        return carry

    lax.fori_loop(0, PER, own_step, 0)

    for copy in table_copies[2:]:
        copy.wait()
    tie_own.wait()
    for dy, dx in AROUND:
        if (dy, dx) != (0, 0):
            first, count = rows_of[-dy]
            part = ties.at[dx + 1, pl.ds(place_of[dy], count), :]

            @pl.when(inside(dy, dx))
            def _():
                arrival(part, tie_sem.at[slot(dy, dx)])

    lane8, sub8 = iota((8, 128), 1), iota((8, 128), 0)

    def limits(pos, count):
        return jnp.where(pos == 0, 0, -SWEEPS), jnp.where(pos == count - 1, NODES, NODES + SWEEPS)

    row_first, row_last = limits(y, n_ty)
    col_first, col_last = limits(x, n_tx)
    picked = []
    for group in range(GROUPS):
        at = pl.ds(group, 8, stride=GROUPS)
        picked.append(jnp.concatenate([ties[1, at, :], jnp.where(lane8 < 64, ties[2, at, :], ties[0, at, :])], axis=1))
    tie = moved(jnp.concatenate(picked, axis=0), take[...])
    for group in range(GROUPS):
        i = sub8 * GROUPS + (group - SWEEPS)
        for u in range(3):
            j = lane8 % 64 * 3 + (u - SWEEPS)
            kept = (i >= row_first) & (i < row_last) & (j >= col_first) & (j < col_last)
            value = tie[group * 8 : (group + 1) * 8, u * 128 : (u + 1) * 128]
            held = jnp.where(kept, 1.0 / (4.0 + value), 0.0)
            rate[group, :, u * 128 : (u + 1) * 128] = held
            pull[group, :, u * 128 : (u + 1) * 128] = value * held

    lag_rows = signed_lag((PATCH, PATCH), 0)

    def softmax_sums(wide, pair, r):
        for q in range(PER):
            score = wide[:, q * PATCH : (q + 1) * PATCH]
            weight = jnp.exp2(score - jnp.max(score))
            at = pl.ds(q * PER + r, 1)
            sums[pair, 0, at, :] = jnp.sum(weight, axis=0, keepdims=True)
            sums[pair, 1, at, :] = jnp.sum(weight * lag_rows, axis=0, keepdims=True)

    def band_step(r, carry):
        arrival(before.at[r], before_sem.at[r])
        arrival(after.at[r], after_sem.at[r])
        pair = paired_spectrum(before[r], left, right_pair)
        there = packed_spectrum(after[r], left, right)
        near = scores(cross_spectrum(pair, spectra[r]), back_right, back_left)
        far = scores(cross_spectrum(pair, there), back_right, back_left)
        softmax_sums(near, 0, r)
        softmax_sums(far, 1, r)
        return carry

    lax.fori_loop(0, PER, band_step, 0)

    lag_lanes = signed_lag((PER * PER, PATCH), 1)
    col_of = iota((PER * PER, 128), 1) - iota((PER * PER, 128), 0) // PER

    def flow(pair):
        weight = sums[pair, 0]
        scale = (1.0 / STRIDE) / jnp.sum(weight, axis=1, keepdims=True)
        rows = jnp.sum(sums[pair, 1], axis=1, keepdims=True) * scale
        cols = jnp.sum(weight * lag_lanes, axis=1, keepdims=True) * scale
        return rows, cols

    def patch_tile(rows, cols):
        part = jnp.where(col_of == 0, rows, jnp.where(col_of == PER, cols, 0.0))
        part = part[:8] + part[8:]
        return part + pltpu.roll(part, 4, 0)

    near, far = flow(0), flow(1)
    near_scale = jnp.where(g >= 2, 0.5, 1.0).astype(f32)
    for kind, flows in ((1, [0.5 * (b - a) for a, b in zip(near, far)]), (0, [near_scale * v for v in near])):
        tile = patch_tile(*flows)
        for d in range(3):
            value = tile if d == 0 else pltpu.roll(tile, 8 * d, 1)
            patch_out[kind, d] = value
            if (kind, d) == (0, 1):
                patch_in[slot(0, 0)] = value

    def patch_copy(kind, dy, dx):
        to = 9 * kind + slot(-dy, -dx)
        return remote(
            patch_out.at[kind, 1 - dx], patch_in.at[to], patch_sent.at[to], patch_sem.at[to],
            (g + kind, y + dy, x + dx),
        )

    ahead = (g >= 1) & (g < n_gz - 1)
    for dy, dx in sorted(AROUND, key=lambda d: -abs(d[0]) - abs(d[1])):

        @pl.when(inside(dy, dx) & ahead)
        def _():
            patch_copy(1, dy, dx).start()

        if (dy, dx) != (0, 0):

            @pl.when(inside(dy, dx))
            def _():
                patch_copy(0, dy, dx).start()

    for dy, dx in AROUND:

        @pl.when(inside(dy, dx) & (g >= 2))
        def _():
            arrival(patch_in.at[9 + slot(dy, dx)], patch_sem.at[9 + slot(dy, dx)])

        if (dy, dx) != (0, 0):

            @pl.when(inside(dy, dx))
            def _():
                arrival(patch_in.at[slot(dy, dx)], patch_sem.at[slot(dy, dx)])

    bands = []
    for dy in (-1, 0, 1):
        total = None
        for dx in (-1, 0, 1):
            tile = patch_in[slot(dy, dx)] + patch_in[9 + slot(dy, dx)]
            total = tile if total is None else total + tile
        bands.append(total)
    bands.append(jnp.zeros((8, 128), f32))
    high, middle, low = (v.astype(f32) for v in thirds(jnp.concatenate(bands, axis=0)))
    patches = (high + pltpu.roll(middle, 32, 1)) + pltpu.roll(low, 64, 1)
    parts = thirds(mm(patches.astype(bf16), spread_cols[...]))
    target = mm(spread_rows[...], jnp.concatenate([*parts, jnp.zeros_like(parts[0])], axis=0))
    for group in range(GROUPS):
        value = target[group * 8 : (group + 1) * 8]
        mesh_a[group] = value
        pull[group] = pull[group] * value

    def sweep(src, dst):
        for group in range(GROUPS):
            here = src[group]
            above = pltpu.roll(src[GROUPS - 1], 1, 0) if group == 0 else src[group - 1]
            below = pltpu.roll(src[0], 7, 0) if group == GROUPS - 1 else src[group + 1]
            first, second, third = (here[:, u * 128 : (u + 1) * 128] for u in range(3))
            beside = jnp.concatenate(
                [pltpu.roll(third, 1, 1) + second, first + third, second + pltpu.roll(first, 127, 1)], axis=1
            )
            dst[group] = ((above + below) + beside) * rate[group] + pull[group]

    def two_sweeps(_, carry):
        sweep(mesh_a, mesh_b)
        sweep(mesh_b, mesh_a)
        return carry

    lax.fori_loop(0, SWEEPS // 2, two_sweeps, 0)

    natural = ties
    ordered = moved(jnp.concatenate([mesh_a[group] for group in range(GROUPS)], axis=0), give[...])
    for group in range(GROUPS):
        at = pl.ds(group, 8, stride=GROUPS)
        for c in range(2):
            natural[c, at, :] = ordered[group * 8 : (group + 1) * 8, c * NODES : (c + 1) * NODES]
    rows = natural[0, SWEEPS : SWEEPS + NODES, :]
    cols = natural[1, SWEEPS : SWEEPS + NODES, :]
    land = lambda at: jnp.clip(at, 0.0, NODES - 1.0)
    sub_i, lane_i = iota((NODES, NODES), 0), iota((NODES, NODES), 1)
    col_0 = land(sub_i[:, :1].astype(f32) + jnp.sum(rows, axis=1, keepdims=True) / NODES)
    row_0 = jnp.sum(jnp.where(sub_i == lane_i, col_0, 0.0), axis=0, keepdims=True)
    row_1 = land(lane_i[:1].astype(f32) + jnp.sum(cols, axis=0, keepdims=True) / NODES)
    landing = jnp.where(sub8 == 0, row_0, jnp.where(sub8 == 1, row_1, 0.0))
    land_out[...] = landing

    def land_copy(step):
        return remote(
            land_out, land_in.at[g], land_sent.at[step - 1], land_sem.at[g], (g + step, y, x)
        )

    for step in range(n_gz - 1, 0, -1):

        @pl.when(g + step < n_gz)
        def _():
            land_copy(step).start()

    mesh_out[0] = rows
    mesh_out[1] = cols
    land_all[n_gz] = landing

    for r in range(PER):

        @pl.when(g < n_gz - 1)
        def _():
            to_later(r).wait_send()

        @pl.when(g > 0)
        def _():
            to_earlier(r).wait_send()

    for dy, dx in AROUND:
        if (dy, dx) != (0, 0):

            @pl.when(inside(dy, dx))
            def _():
                tie_copy(dy, dx).wait_send()
                patch_copy(0, dy, dx).wait_send()

        @pl.when(inside(dy, dx) & ahead)
        def _():
            patch_copy(1, dy, dx).wait_send()

    for t in range(n_gz - 1):

        @pl.when(t < g)
        def _():
            arrival(land_in.at[t], land_sem.at[t])

    for t in range(n_gz):
        land_all[t] = land_in[t]

    for step in range(1, n_gz):

        @pl.when(g + step < n_gz)
        def _():
            land_copy(step).wait_send()


def finish(n_gz, mesh_in, land_all, mesh_out, drift_out, sem):
    copy = pltpu.make_async_copy(mesh_in, mesh_out.at[0], sem)
    copy.start()
    sub_i, lane_i = iota((NODES, NODES), 0), iota((NODES, NODES), 1)
    sub_f, lane_f = sub_i.astype(f32), lane_i.astype(f32)
    eye = sub_i == lane_i
    to_row = lambda col: jnp.sum(jnp.where(eye, col, 0.0), axis=0, keepdims=True)
    to_col = lambda row: jnp.sum(jnp.where(eye, row, 0.0), axis=1, keepdims=True)
    for c in range(2):
        value = to_col(land_all[n_gz, c : c + 1, :])
        for t in range(n_gz - 2, -1, -1):
            place = land_all[t, c : c + 1, :]
            if (n_gz - 2 - t) % 2 == 0:
                value = jnp.sum(hat(place - sub_f) * value, axis=0, keepdims=True)
            else:
                value = jnp.sum(hat(to_col(place) - lane_f) * value, axis=1, keepdims=True)
        if n_gz % 2:
            value = to_row(value)
        drift_out[0, 0, 0, c : c + 1, :] = value - lane_f[:1]
    copy.wait()


def solution(mesh):
    sizes = tuple(mesh.shape[name] for name in ("gz", "ty", "tx"))
    n_gz = sizes[0]
    constants = tables()
    dma = pltpu.SemaphoreType.DMA
    vmem = pl.BlockSpec(memory_space=pltpu.VMEM)
    hbm = pl.BlockSpec(memory_space=pltpu.HBM)

    def local(images, boundary, anchor):
        relaxed, landings = pl.pallas_call(
            functools.partial(kernel, sizes),
            out_shape=(
                jax.ShapeDtypeStruct((2, NODES, NODES), f32),
                jax.ShapeDtypeStruct((n_gz + 1, 8, NODES), f32),
            ),
            in_specs=[hbm] * (3 + len(constants)),
            out_specs=(vmem, vmem),
            scratch_shapes=[
                pltpu.VMEM((PER, PATCH, TILE), bf16),
                pltpu.VMEM((PER, PATCH, TILE), bf16),
                pltpu.VMEM((PER, PATCH, TILE), bf16),
                pltpu.VMEM((PER, PER * PATCH, PATCH), f32),
                pltpu.VMEM((3, WIDE, NODES), f32),
                pltpu.VMEM((18, 8, NODES), f32),
                pltpu.VMEM((2, 3, 8, NODES), f32),
                pltpu.VMEM((2, 2, PER * PER, PATCH), f32),
                pltpu.VMEM((n_gz, 8, NODES), f32),
                pltpu.VMEM((8, NODES), f32),
                pltpu.VMEM((GROUPS, 8, LANES), f32),
                pltpu.VMEM((GROUPS, 8, LANES), f32),
                pltpu.VMEM((GROUPS, 8, LANES), f32),
                pltpu.VMEM((GROUPS, 8, LANES), f32),
                *(pltpu.VMEM(c.shape, bf16) for c in constants),
                dma((len(constants),)),
                dma((PER,)),
                dma((PER,)),
                dma((PER,)),
                dma((PER,)),
                dma((PER,)),
                dma((9,)),
                dma((9,)),
                dma((18,)),
                dma((18,)),
                dma((n_gz,)),
                dma((n_gz,)),
            ],
            compiler_params=pltpu.CompilerParams(
                collective_id=0, has_side_effects=True, vmem_limit_bytes=GRANT
            ),
            name="align",
        )(*(pltpu.with_memory_space_constraint(v, pltpu.HBM) for v in (images, boundary, anchor, *map(jnp.asarray, constants))))
        return pl.pallas_call(
            functools.partial(finish, n_gz),
            out_shape=(
                jax.ShapeDtypeStruct((1, 2, NODES, NODES), f32),
                jax.ShapeDtypeStruct((1, 1, 1, 2, NODES), f32),
            ),
            in_specs=[vmem, vmem],
            out_specs=(hbm, vmem),
            scratch_shapes=[dma],
            compiler_params=pltpu.CompilerParams(vmem_limit_bytes=4 * 1024 * 1024),
            name="finish",
        )(relaxed, landings)

    return jax.shard_map(
        local,
        mesh=mesh,
        in_specs=(P("gz", "ty", "tx"), P("ty", "tx"), P("gz", "ty", "tx")),
        out_specs=(P("gz", None, "ty", "tx"), P("gz", "ty", "tx", None, None)),
        check_vma=False,
    )
```

```python
import functools
import math

import jax
import jax.numpy as jnp
import numpy as np
from jax import lax
from jax.experimental import pallas as pl
from jax.experimental.pallas import tpu as pltpu
from jax.sharding import PartitionSpec as P

PATCH = 128
STRIDE = 4
SWEEPS = 32
TILE = 512
NODES = 128
PER = TILE // PATCH
Q = 4
WIDTH = Q * PATCH
PIECES = PER * PER // Q
WIDE = NODES + 2 * SWEEPS
GROUPS = WIDE // 8
LANES = 2 * WIDE

GRANT = 48 * 1024 * 1024

f32 = jnp.float32
bf16 = jnp.bfloat16
MESH = pl.DeviceIdType.MESH
AROUND = [(dy, dx) for dy in (-1, 0, 1) for dx in (-1, 0, 1)]
SIDES = [(-1, 0), (1, 0), (0, -1), (0, 1)]
CORNERS = [(-1, -1), (-1, 1), (1, -1), (1, 1)]


def slot(dy, dx):
    return (dy + 1) * 3 + dx + 1


def pieces(table, count):
    parts = []
    rest = np.asarray(table, np.float64)
    for _ in range(count):
        part = rest.astype(jnp.bfloat16)
        parts.append(part)
        rest = rest - part.astype(np.float64)
    return parts


def spread_table():
    pos = (np.arange(NODES) + 0.5) * STRIDE / PATCH - 0.5
    weights = np.maximum(0.0, 1.0 - np.abs(pos[:, None] - np.arange(PER)[None, :]))
    return weights / weights.sum(axis=1, keepdims=True)


def tables():
    half = PATCH // 2
    n = np.arange(PATCH)
    angle = lambda k: 2.0 * np.pi * (n[:, None] * k[None, :] % PATCH) / PATCH
    low, high = np.arange(half), np.arange(1, half)
    cos_low, sin_high = np.cos(angle(low)), np.sin(angle(high))
    last = np.cos(np.pi * n)[:, None]
    zero = np.zeros_like(last)
    basis = np.concatenate([cos_low, last, sin_high], axis=1)
    same = np.concatenate([cos_low, last, cos_low[:, 1:]], axis=1)
    cross = np.concatenate([zero, sin_high, zero, -sin_high], axis=1)
    weight = np.full(PATCH, 2.0 / PATCH)
    weight[[0, half]] = 1.0 / PATCH
    inverse = basis * weight[None, :]

    b_hi, b_lo = pieces(basis, 2)
    s_hi, s_lo = pieces(same, 2)
    c_hi, c_lo = pieces(cross, 2)
    r_hi, r_lo = pieces(inverse.T, 2)
    l_hi, l_lo = pieces(inverse * (math.log2(math.e) / PATCH), 2)
    left = np.concatenate([b_hi.T, b_lo.T], axis=0)
    right = np.concatenate([b_hi, b_lo], axis=1)
    right_pair = np.concatenate([s_hi, c_hi, s_lo, c_lo], axis=1)
    back_right = np.concatenate([r_hi, r_lo], axis=1)
    back_left = np.concatenate([l_hi, l_lo], axis=0)
    twice = lambda t, axis: np.concatenate([t, t], axis=axis)

    spread = spread_table()
    rows = np.zeros((WIDE, 128))
    for group in range(GROUPS):
        for sub in range(8):
            i = sub * GROUPS + group - SWEEPS
            dy = i // NODES
            for piece in range(3):
                first = piece * 32 + (dy + 1) * 8
                rows[group * 8 + sub, first : first + PER] = spread[i - dy * NODES]
    cols = np.zeros((128, LANES))
    take = np.zeros((256, LANES))
    give = np.zeros((LANES, 2 * NODES))
    for u in range(3):
        for lane in range(128):
            comp, j = lane // 64, lane % 64 * 3 + u - SWEEPS
            dx = j // NODES
            at = u * 128 + lane
            for piece in range(3):
                first = piece * 32 + (dx + 1) * 8 + comp * PER
                cols[first : first + PER, at] = spread[j - dx * NODES]
            take[j if dx == 0 else 128 + j % NODES, at] = 1.0
            if dx == 0:
                give[at, comp * NODES + j] = 1.0
    return tuple(
        t.astype(jnp.bfloat16)
        for t in (
            left,
            twice(right, 0),
            twice(right_pair, 0),
            twice(back_right, 0),
            twice(back_left, 1),
            take,
            cols,
            rows,
            give,
        )
    )


def mm(a, b):
    return jnp.dot(a, b, preferred_element_type=f32)


def halves(value):
    hi = value.astype(bf16)
    return hi, (value - hi.astype(f32)).astype(bf16)


def iota(shape, dim):
    return lax.broadcasted_iota(jnp.int32, shape, dim)


def stacked_rows(wide):
    return jnp.concatenate([wide[:, q * PATCH : (q + 1) * PATCH] for q in range(wide.shape[1] // PATCH)], axis=0)


def side_by_side(tall):
    return jnp.concatenate([tall[q * PATCH : (q + 1) * PATCH] for q in range(tall.shape[0] // PATCH)], axis=1)


def row_pass(pixels, left):
    both = mm(left[...], pixels)
    return jnp.concatenate(halves(stacked_rows(both[:PATCH] + both[PATCH:])), axis=1)


def packed_spectrum(pixels, left, right):
    both = mm(row_pass(pixels, left), right[...])
    return both[:, :PATCH] + both[:, PATCH:]


def paired_spectrum(pixels, left, right_pair):
    both = mm(row_pass(pixels, left), right_pair[...])
    return (
        both[:, :PATCH] + both[:, 2 * PATCH : 3 * PATCH],
        both[:, PATCH : 2 * PATCH] + both[:, 3 * PATCH :],
    )


def cross_spectrum(pair, later):
    half = PATCH // 2
    same, cross = pair
    turned = pltpu.roll(later, half, 1)
    first = iota((half, PATCH), 0) == 0
    out = []
    for q in range(Q):
        top = slice(q * PATCH, q * PATCH + half)
        low = slice(q * PATCH + half, (q + 1) * PATCH)
        joint = lambda e, c: same[e] * later[c] + cross[e] * turned[c]
        low_low = joint(low, low)
        out.append(joint(top, top) + jnp.where(first, 0.0, low_low))
        out.append(jnp.where(first, low_low, joint(top, low) - joint(low, top)))
    return jnp.concatenate(out, axis=0)


def scores(product, back_right, back_left):
    both = mm(jnp.concatenate(halves(product), axis=1), back_right[...])
    wide = side_by_side(both[:, :PATCH] + both[:, PATCH:])
    both = mm(back_left[...], jnp.concatenate(halves(wide), axis=0))
    return both[:PATCH] + both[PATCH:]


def signed_lag(shape, dim):
    lag = iota(shape, dim)
    return jnp.where(lag < PATCH // 2, lag, lag - PATCH).astype(f32)


def hat(offset):
    return jnp.maximum(0.0, 1.0 - jnp.abs(offset))


def thirds(value):
    high = value.astype(bf16)
    rest = value - high.astype(f32)
    middle = rest.astype(bf16)
    return high, middle, (rest - middle.astype(f32)).astype(bf16)


def moved(value, selection):
    count = value.shape[0]
    parts = mm(jnp.concatenate(thirds(value), axis=0), selection)
    return parts[:count] + parts[count : 2 * count] + parts[2 * count :]


def kernel(
    sizes,
    images, boundary, anchor, *rest,
):
    n_gz, n_ty, n_tx = sizes
    tables_in, rest = rest[:9], rest[9:]
    (
        mesh_out, land_all,
        own, before, after, spectra, ties, patch_in, patch_out, sums, land_in, land_out,
        rate, pull, mesh_a, mesh_b,
    ) = rest[:16]
    tables_here, rest = rest[16:25], rest[25:]
    (
        table_sem, own_sem, before_sem, after_sem, up_sem, down_sem, tie_sem, tie_sent,
        patch_sem, patch_sent, land_sem, land_sent, rounds,
    ) = rest
    left, right, right_pair, back_right, back_left, take, spread_cols, spread_rows, give = tables_here
    g, y, x = lax.axis_index("gz"), lax.axis_index("ty"), lax.axis_index("tx")

    def inside(dy, dx):
        ok = None
        for pos, step, count in ((y, dy, n_ty), (x, dx, n_tx)):
            if step:
                here = (pos + step >= 0) & (pos + step < count)
                ok = here if ok is None else ok & here
        return (g >= 0) if ok is None else ok

    def told(semaphore, ok, device):
        @pl.when(ok)
        def _():
            pl.semaphore_signal(semaphore, inc=1, device_id=device, device_id_type=MESH)

        return jnp.where(ok, 1, 0).astype(jnp.int32)

    def within(step):
        return (g + step >= 0) & (g + step < n_gz)

    near = [(within(dz), (g + dz, y, x)) for dz in (-1, 1)]
    near += [(inside(dy, dx), (g, y + dy, x + dx)) for dy, dx in SIDES]

    barrier = pltpu.get_barrier_semaphore()
    greeted = jnp.int32(0)
    for ok, device in near:
        greeted += told(barrier, ok, device)

    def band(ref, k):
        rows = pl.ds(pl.multiple_of(k // (PER // Q) * PATCH, PATCH), PATCH)
        return ref.at[rows, pl.ds(pl.multiple_of(k % (PER // Q) * WIDTH, WIDTH), WIDTH)]

    table_copies = [
        pltpu.make_async_copy(src, dst, table_sem.at[i])
        for i, (src, dst) in enumerate(zip(tables_in, tables_here))
    ]
    for copy in table_copies[:2]:
        copy.start()
    for r in range(PIECES):
        pltpu.make_async_copy(band(images.at[0], r), own.at[r], own_sem.at[r]).start()
    for copy in table_copies[2:]:
        copy.start()
    tie_own = pltpu.make_async_copy(
        anchor.at[0], ties.at[1, pl.ds(SWEEPS, NODES), :], tie_sem.at[slot(0, 0)]
    )
    tie_own.start()
    for r in range(PIECES):

        @pl.when(g == 0)
        def _():
            pltpu.make_async_copy(band(boundary, r), before.at[r], before_sem.at[r]).start()

        @pl.when(g == n_gz - 1)
        def _():
            pltpu.make_async_copy(band(boundary, r), after.at[r], after_sem.at[r]).start()

    pl.semaphore_wait(barrier, greeted)

    def remote(src, dst, sent, arrived, device):
        return pltpu.make_async_remote_copy(
            src_ref=src, dst_ref=dst, send_sem=sent, recv_sem=arrived, device_id=device, device_id_type=MESH
        )

    def to_later(r):
        return remote(band(images.at[0], r), before.at[r], up_sem.at[r], before_sem.at[r], (g + 1, y, x))

    def to_earlier(r):
        return remote(band(images.at[0], r), after.at[r], down_sem.at[r], after_sem.at[r], (g - 1, y, x))

    for r in range(PIECES):

        @pl.when(g < n_gz - 1)
        def _():
            to_later(r).start()

        @pl.when(g > 0)
        def _():
            to_earlier(r).start()

    rows_of = {-1: (0, SWEEPS), 0: (0, NODES), 1: (NODES - SWEEPS, SWEEPS)}
    place_of = {-1: 0, 0: SWEEPS, 1: SWEEPS + NODES}

    def tie_copy(dy, dx):
        first, count = rows_of[dy]
        to = slot(-dy, -dx)
        return remote(
            anchor.at[0, pl.ds(first, count), :],
            ties.at[1 - dx, pl.ds(place_of[-dy], count), :],
            tie_sent.at[to],
            tie_sem.at[to],
            (g, y + dy, x + dx),
        )

    def send_ties(steps):
        for dy, dx in steps:

            @pl.when(inside(dy, dx))
            def _():
                tie_copy(dy, dx).start()

    send_ties(SIDES)
    passed = jnp.int32(0)
    for ok, device in near:
        passed += told(rounds.at[0], ok, device)

    ramp_rows = iota((8, NODES), 1).astype(f32)
    for t in range(n_gz):

        @pl.when(t >= g)
        def _():
            land_in[t] = ramp_rows

    for edge, count, first in ((y == 0, SWEEPS, 0), (y == n_ty - 1, SWEEPS, SWEEPS + NODES)):

        @pl.when(edge)
        def _():
            for d in range(3):
                ties[d, pl.ds(first, count), :] = jnp.zeros((count, NODES), f32)

    for edge, d in ((x == 0, 0), (x == n_tx - 1, 2)):

        @pl.when(edge)
        def _():
            ties[d] = jnp.zeros((WIDE, NODES), f32)

    for dy, dx in AROUND:
        if (dy, dx) != (0, 0):

            @pl.when(jnp.logical_not(inside(dy, dx)))
            def _():
                patch_in[slot(dy, dx)] = jnp.zeros((8, NODES), f32)

        @pl.when(jnp.logical_not(inside(dy, dx)) | (g < 2))
        def _():
            patch_in[9 + slot(dy, dx)] = jnp.zeros((8, NODES), f32)

    def arrival(ref, sem):
        pltpu.make_async_copy(ref, ref, sem).wait()

    for copy in table_copies[:2]:
        copy.wait()

    def own_step(r, carry):
        arrival(own.at[r], own_sem.at[r])
        spectra[r] = packed_spectrum(own[r], left, right)
        return carry

    lax.fori_loop(0, PIECES // 2, own_step, 0)
    pl.semaphore_wait(rounds.at[0], passed)
    send_ties(CORNERS)
    passed_on = jnp.int32(0)
    for step in (-2, -1, 1, 2):
        passed_on += told(rounds.at[1], within(step), (g + step, y, x))
    lax.fori_loop(PIECES // 2, PIECES, own_step, 0)
    pl.semaphore_wait(rounds.at[1], passed_on)
    told(rounds.at[2], within(-4), (g - 4, y, x))

    for copy in table_copies[2:]:
        copy.wait()

    lag_rows = signed_lag((PATCH, PATCH), 0)

    def softmax_sums(wide, k):
        for at_pair in range(2 * Q):
            pair, q = at_pair // Q, at_pair % Q
            score = wide[:, at_pair * PATCH : (at_pair + 1) * PATCH]
            weight = jnp.exp2(score - jnp.max(score))
            at = pl.ds((k % (PER // Q) * Q + q) * PER + k // (PER // Q), 1)
            sums[pair, 0, at, :] = jnp.sum(weight, axis=0, keepdims=True)
            sums[pair, 1, at, :] = jnp.sum(weight * lag_rows, axis=0, keepdims=True)

    def band_step(k, carry):
        arrival(before.at[k], before_sem.at[k])
        arrival(after.at[k], after_sem.at[k])
        pair = paired_spectrum(before[k], left, right_pair)
        there = packed_spectrum(after[k], left, right)
        products = [cross_spectrum(pair, spectra[k]), cross_spectrum(pair, there)]
        softmax_sums(scores(jnp.concatenate(products, axis=0), back_right, back_left), k)
        return carry

    lax.fori_loop(0, PIECES, band_step, 0)

    lag_lanes = signed_lag((PER * PER, PATCH), 1)
    col_of = iota((PER * PER, 128), 1) - iota((PER * PER, 128), 0) // PER

    def flow(pair):
        weight = sums[pair, 0]
        scale = (1.0 / STRIDE) / jnp.sum(weight, axis=1, keepdims=True)
        rows = jnp.sum(sums[pair, 1], axis=1, keepdims=True) * scale
        cols = jnp.sum(weight * lag_lanes, axis=1, keepdims=True) * scale
        return rows, cols

    def patch_tile(rows, cols):
        part = jnp.where(col_of == 0, rows, jnp.where(col_of == PER, cols, 0.0))
        part = part[:8] + part[8:]
        return part + pltpu.roll(part, 4, 0)

    nearer, farther = flow(0), flow(1)
    near_scale = jnp.where(g >= 2, 0.5, 1.0).astype(f32)
    for kind, flows in ((1, [0.5 * (b - a) for a, b in zip(nearer, farther)]), (0, [near_scale * v for v in nearer])):
        tile = patch_tile(*flows)
        for d in range(3):
            value = tile if d == 0 else pltpu.roll(tile, 8 * d, 1)
            patch_out[kind, d] = value
            if (kind, d) == (0, 1):
                patch_in[slot(0, 0)] = value

    def patch_copy(kind, dy, dx):
        to = 9 * kind + slot(-dy, -dx)
        return remote(
            patch_out.at[kind, 1 - dx], patch_in.at[to], patch_sent.at[to], patch_sem.at[to],
            (g + kind, y + dy, x + dx),
        )

    ahead = (g >= 1) & (g < n_gz - 1)
    for dy, dx in sorted(AROUND, key=lambda d: -abs(d[0]) - abs(d[1])):

        @pl.when(inside(dy, dx) & ahead)
        def _():
            patch_copy(1, dy, dx).start()

        if (dy, dx) != (0, 0):

            @pl.when(inside(dy, dx))
            def _():
                patch_copy(0, dy, dx).start()

    tie_own.wait()
    for dy, dx in AROUND:
        if (dy, dx) != (0, 0):
            first, count = rows_of[-dy]
            part = ties.at[dx + 1, pl.ds(place_of[dy], count), :]

            @pl.when(inside(dy, dx))
            def _():
                arrival(part, tie_sem.at[slot(dy, dx)])

    lane8, sub8 = iota((8, 128), 1), iota((8, 128), 0)

    def limits(pos, count):
        return jnp.where(pos == 0, 0, -SWEEPS), jnp.where(pos == count - 1, NODES, NODES + SWEEPS)

    row_first, row_last = limits(y, n_ty)
    col_first, col_last = limits(x, n_tx)
    picked = []
    for group in range(GROUPS):
        at = pl.ds(group, 8, stride=GROUPS)
        picked.append(jnp.concatenate([ties[1, at, :], jnp.where(lane8 < 64, ties[2, at, :], ties[0, at, :])], axis=1))
    tie = moved(jnp.concatenate(picked, axis=0), take[...])
    for group in range(GROUPS):
        i = sub8 * GROUPS + (group - SWEEPS)
        for u in range(3):
            j = lane8 % 64 * 3 + (u - SWEEPS)
            kept = (i >= row_first) & (i < row_last) & (j >= col_first) & (j < col_last)
            value = tie[group * 8 : (group + 1) * 8, u * 128 : (u + 1) * 128]
            held = jnp.where(kept, 1.0 / (4.0 + value), 0.0)
            rate[group, :, u * 128 : (u + 1) * 128] = held
            pull[group, :, u * 128 : (u + 1) * 128] = value * held

    @pl.when(within(4))
    def _():
        pl.semaphore_wait(rounds.at[2], 1)

    for dy, dx in AROUND:

        @pl.when(inside(dy, dx) & (g >= 2))
        def _():
            arrival(patch_in.at[9 + slot(dy, dx)], patch_sem.at[9 + slot(dy, dx)])

        if (dy, dx) != (0, 0):

            @pl.when(inside(dy, dx))
            def _():
                arrival(patch_in.at[slot(dy, dx)], patch_sem.at[slot(dy, dx)])

    bands = []
    for dy in (-1, 0, 1):
        total = None
        for dx in (-1, 0, 1):
            tile = patch_in[slot(dy, dx)] + patch_in[9 + slot(dy, dx)]
            total = tile if total is None else total + tile
        bands.append(total)
    bands.append(jnp.zeros((8, 128), f32))
    high, middle, low = (v.astype(f32) for v in thirds(jnp.concatenate(bands, axis=0)))
    patches = (high + pltpu.roll(middle, 32, 1)) + pltpu.roll(low, 64, 1)
    parts = thirds(mm(patches.astype(bf16), spread_cols[...]))
    target = mm(spread_rows[...], jnp.concatenate([*parts, jnp.zeros_like(parts[0])], axis=0))
    for group in range(GROUPS):
        value = target[group * 8 : (group + 1) * 8]
        mesh_a[group] = value
        pull[group] = pull[group] * value

    def sweep(src, dst):
        for group in range(GROUPS):
            here = src[group]
            above = pltpu.roll(src[GROUPS - 1], 1, 0) if group == 0 else src[group - 1]
            below = pltpu.roll(src[0], 7, 0) if group == GROUPS - 1 else src[group + 1]
            first, second, third = (here[:, u * 128 : (u + 1) * 128] for u in range(3))
            beside = jnp.concatenate(
                [pltpu.roll(third, 1, 1) + second, first + third, second + pltpu.roll(first, 127, 1)], axis=1
            )
            dst[group] = ((above + below) + beside) * rate[group] + pull[group]

    def two_sweeps(_, carry):
        sweep(mesh_a, mesh_b)
        sweep(mesh_b, mesh_a)
        return carry

    lax.fori_loop(0, SWEEPS // 2, two_sweeps, 0)

    natural = ties
    ordered = moved(jnp.concatenate([mesh_a[group] for group in range(GROUPS)], axis=0), give[...])
    for group in range(GROUPS):
        at = pl.ds(group, 8, stride=GROUPS)
        for c in range(2):
            natural[c, at, :] = ordered[group * 8 : (group + 1) * 8, c * NODES : (c + 1) * NODES]
    rows = natural[0, SWEEPS : SWEEPS + NODES, :]
    cols = natural[1, SWEEPS : SWEEPS + NODES, :]
    land = lambda at: jnp.clip(at, 0.0, NODES - 1.0)
    sub_i, lane_i = iota((NODES, NODES), 0), iota((NODES, NODES), 1)
    col_0 = land(sub_i[:, :1].astype(f32) + jnp.sum(rows, axis=1, keepdims=True) / NODES)
    row_0 = jnp.sum(jnp.where(sub_i == lane_i, col_0, 0.0), axis=0, keepdims=True)
    row_1 = land(lane_i[:1].astype(f32) + jnp.sum(cols, axis=0, keepdims=True) / NODES)
    landing = jnp.where(sub8 == 0, row_0, jnp.where(sub8 == 1, row_1, 0.0))
    land_out[...] = landing

    def land_copy(step):
        return remote(
            land_out, land_in.at[g], land_sent.at[step - 1], land_sem.at[g], (g + step, y, x)
        )

    for step in range(n_gz - 1, 0, -1):

        @pl.when(g + step < n_gz)
        def _():
            land_copy(step).start()

    mesh_out[0] = rows
    mesh_out[1] = cols
    land_all[n_gz] = landing

    for r in range(PIECES):

        @pl.when(g < n_gz - 1)
        def _():
            to_later(r).wait_send()

        @pl.when(g > 0)
        def _():
            to_earlier(r).wait_send()

    for dy, dx in AROUND:
        if (dy, dx) != (0, 0):

            @pl.when(inside(dy, dx))
            def _():
                tie_copy(dy, dx).wait_send()
                patch_copy(0, dy, dx).wait_send()

        @pl.when(inside(dy, dx) & ahead)
        def _():
            patch_copy(1, dy, dx).wait_send()

    for t in range(n_gz - 1):

        @pl.when(t < g)
        def _():
            arrival(land_in.at[t], land_sem.at[t])

    for t in range(n_gz):
        land_all[t] = land_in[t]

    for step in range(1, n_gz):

        @pl.when(g + step < n_gz)
        def _():
            land_copy(step).wait_send()


def finish(n_gz, mesh_in, land_all, mesh_out, drift_out, sem):
    copy = pltpu.make_async_copy(mesh_in, mesh_out.at[0], sem)
    copy.start()
    sub_i, lane_i = iota((NODES, NODES), 0), iota((NODES, NODES), 1)
    sub_f, lane_f = sub_i.astype(f32), lane_i.astype(f32)
    eye = sub_i == lane_i
    to_row = lambda col: jnp.sum(jnp.where(eye, col, 0.0), axis=0, keepdims=True)
    to_col = lambda row: jnp.sum(jnp.where(eye, row, 0.0), axis=1, keepdims=True)
    for c in range(2):
        value = to_col(land_all[n_gz, c : c + 1, :])
        for t in range(n_gz - 2, -1, -1):
            place = land_all[t, c : c + 1, :]
            if (n_gz - 2 - t) % 2 == 0:
                value = jnp.sum(hat(place - sub_f) * value, axis=0, keepdims=True)
            else:
                value = jnp.sum(hat(to_col(place) - lane_f) * value, axis=1, keepdims=True)
        if n_gz % 2:
            value = to_row(value)
        drift_out[0, 0, 0, c : c + 1, :] = value - lane_f[:1]
    copy.wait()


def solution(mesh):
    sizes = tuple(mesh.shape[name] for name in ("gz", "ty", "tx"))
    n_gz = sizes[0]
    constants = tables()
    dma = pltpu.SemaphoreType.DMA
    vmem = pl.BlockSpec(memory_space=pltpu.VMEM)
    hbm = pl.BlockSpec(memory_space=pltpu.HBM)

    def local(images, boundary, anchor):
        relaxed, landings = pl.pallas_call(
            functools.partial(kernel, sizes),
            out_shape=(
                jax.ShapeDtypeStruct((2, NODES, NODES), f32),
                jax.ShapeDtypeStruct((n_gz + 1, 8, NODES), f32),
            ),
            in_specs=[hbm] * (3 + len(constants)),
            out_specs=(vmem, vmem),
            scratch_shapes=[
                pltpu.VMEM((PIECES, PATCH, WIDTH), bf16),
                pltpu.VMEM((PIECES, PATCH, WIDTH), bf16),
                pltpu.VMEM((PIECES, PATCH, WIDTH), bf16),
                pltpu.VMEM((PIECES, WIDTH, PATCH), f32),
                pltpu.VMEM((3, WIDE, NODES), f32),
                pltpu.VMEM((18, 8, NODES), f32),
                pltpu.VMEM((2, 3, 8, NODES), f32),
                pltpu.VMEM((2, 2, PER * PER, PATCH), f32),
                pltpu.VMEM((n_gz, 8, NODES), f32),
                pltpu.VMEM((8, NODES), f32),
                pltpu.VMEM((GROUPS, 8, LANES), f32),
                pltpu.VMEM((GROUPS, 8, LANES), f32),
                pltpu.VMEM((GROUPS, 8, LANES), f32),
                pltpu.VMEM((GROUPS, 8, LANES), f32),
                *(pltpu.VMEM(c.shape, bf16) for c in constants),
                dma((len(constants),)),
                dma((PIECES,)),
                dma((PIECES,)),
                dma((PIECES,)),
                dma((PIECES,)),
                dma((PIECES,)),
                dma((9,)),
                dma((9,)),
                dma((18,)),
                dma((18,)),
                dma((n_gz,)),
                dma((n_gz,)),
                pltpu.SemaphoreType.REGULAR((3,)),
            ],
            compiler_params=pltpu.CompilerParams(
                collective_id=0, has_side_effects=True, vmem_limit_bytes=GRANT
            ),
            name="align",
        )(*(pltpu.with_memory_space_constraint(v, pltpu.HBM) for v in (images, boundary, anchor, *map(jnp.asarray, constants))))
        return pl.pallas_call(
            functools.partial(finish, n_gz),
            out_shape=(
                jax.ShapeDtypeStruct((1, 2, NODES, NODES), f32),
                jax.ShapeDtypeStruct((1, 1, 1, 2, NODES), f32),
            ),
            in_specs=[vmem, vmem],
            out_specs=(hbm, vmem),
            scratch_shapes=[dma],
            compiler_params=pltpu.CompilerParams(vmem_limit_bytes=4 * 1024 * 1024),
            name="finish",
        )(relaxed, landings)

    return jax.shard_map(
        local,
        mesh=mesh,
        in_specs=(P("gz", "ty", "tx"), P("ty", "tx"), P("gz", "ty", "tx")),
        out_specs=(P("gz", None, "ty", "tx"), P("gz", "ty", "tx", None, None)),
        check_vma=False,
    )
```

```python
import functools
import math

import jax
import jax.numpy as jnp
import numpy as np
from jax import lax
from jax.experimental import pallas as pl
from jax.experimental.pallas import tpu as pltpu
from jax.sharding import PartitionSpec as P

PATCH = 128
STRIDE = 4
SWEEPS = 32
TILE = 512
NODES = 128
PER = TILE // PATCH
Q = 4
WIDTH = Q * PATCH
PIECES = PER * PER // Q
WIDE = NODES + 2 * SWEEPS
GROUPS = WIDE // 8
LANES = 2 * WIDE

GRANT = 48 * 1024 * 1024

f32 = jnp.float32
bf16 = jnp.bfloat16
MESH = pl.DeviceIdType.MESH
AROUND = [(dy, dx) for dy in (-1, 0, 1) for dx in (-1, 0, 1)]
SIDES = [(-1, 0), (1, 0), (0, -1), (0, 1)]
CORNERS = [(-1, -1), (-1, 1), (1, -1), (1, 1)]


def slot(dy, dx):
    return (dy + 1) * 3 + dx + 1


def pieces(table, count):
    parts = []
    rest = np.asarray(table, np.float64)
    for _ in range(count):
        part = rest.astype(jnp.bfloat16)
        parts.append(part)
        rest = rest - part.astype(np.float64)
    return parts


def spread_table():
    pos = (np.arange(NODES) + 0.5) * STRIDE / PATCH - 0.5
    weights = np.maximum(0.0, 1.0 - np.abs(pos[:, None] - np.arange(PER)[None, :]))
    return weights / weights.sum(axis=1, keepdims=True)


def tables():
    half = PATCH // 2
    n = np.arange(PATCH)
    angle = lambda k: 2.0 * np.pi * (n[:, None] * k[None, :] % PATCH) / PATCH
    low, high = np.arange(half), np.arange(1, half)
    cos_low, sin_high = np.cos(angle(low)), np.sin(angle(high))
    last = np.cos(np.pi * n)[:, None]
    zero = np.zeros_like(last)
    basis = np.concatenate([cos_low, last, sin_high], axis=1)
    same = np.concatenate([cos_low, last, cos_low[:, 1:]], axis=1)
    cross = np.concatenate([zero, sin_high, zero, -sin_high], axis=1)
    weight = np.full(PATCH, 2.0 / PATCH)
    weight[[0, half]] = 1.0 / PATCH
    inverse = basis * weight[None, :]

    b_hi, b_lo = pieces(basis, 2)
    s_hi, s_lo = pieces(same, 2)
    c_hi, c_lo = pieces(cross, 2)
    r_hi, r_lo = pieces(inverse.T, 2)
    l_hi, l_lo = pieces(inverse * (math.log2(math.e) / PATCH), 2)
    left = np.concatenate([b_hi.T, b_lo.T], axis=0)
    right = np.concatenate([b_hi, b_lo], axis=1)
    right_pair = np.concatenate([s_hi, c_hi, s_lo, c_lo], axis=1)
    back_right = np.concatenate([r_hi, r_lo], axis=1)
    back_left = np.concatenate([l_hi, l_lo], axis=0)
    twice = lambda t, axis: np.concatenate([t, t], axis=axis)

    spread = spread_table()
    rows = np.zeros((WIDE, 128))
    for group in range(GROUPS):
        for sub in range(8):
            i = sub * GROUPS + group - SWEEPS
            dy = i // NODES
            for piece in range(3):
                first = piece * 32 + (dy + 1) * 8
                rows[group * 8 + sub, first : first + PER] = spread[i - dy * NODES]
    cols = np.zeros((128, LANES))
    take = np.zeros((256, LANES))
    give = np.zeros((LANES, 2 * NODES))
    for u in range(3):
        for lane in range(128):
            comp, j = lane // 64, lane % 64 * 3 + u - SWEEPS
            dx = j // NODES
            at = u * 128 + lane
            for piece in range(3):
                first = piece * 32 + (dx + 1) * 8 + comp * PER
                cols[first : first + PER, at] = spread[j - dx * NODES]
            take[j if dx == 0 else 128 + j % NODES, at] = 1.0
            if dx == 0:
                give[at, comp * NODES + j] = 1.0
    return tuple(
        t.astype(jnp.bfloat16)
        for t in (
            left,
            twice(right, 0),
            twice(right_pair, 0),
            twice(back_right, 0),
            twice(back_left, 1),
            take,
            cols,
            rows,
            give,
        )
    )


def mm(a, b):
    return jnp.dot(a, b, preferred_element_type=f32)


def halves(value):
    hi = value.astype(bf16)
    return hi, (value - hi.astype(f32)).astype(bf16)


def iota(shape, dim):
    return lax.broadcasted_iota(jnp.int32, shape, dim)


def stacked_rows(wide):
    return jnp.concatenate([wide[:, q * PATCH : (q + 1) * PATCH] for q in range(wide.shape[1] // PATCH)], axis=0)


def side_by_side(tall):
    return jnp.concatenate([tall[q * PATCH : (q + 1) * PATCH] for q in range(tall.shape[0] // PATCH)], axis=1)


def row_pass(pixels, left):
    both = mm(left[...], pixels)
    return jnp.concatenate(halves(stacked_rows(both[:PATCH] + both[PATCH:])), axis=1)


def packed_spectrum(pixels, left, right):
    both = mm(row_pass(pixels, left), right[...])
    return both[:, :PATCH] + both[:, PATCH:]


def paired_spectrum(pixels, left, right_pair):
    both = mm(row_pass(pixels, left), right_pair[...])
    return (
        both[:, :PATCH] + both[:, 2 * PATCH : 3 * PATCH],
        both[:, PATCH : 2 * PATCH] + both[:, 3 * PATCH :],
    )


def cross_spectrum(pair, later):
    half = PATCH // 2
    same, cross = pair
    turned = pltpu.roll(later, half, 1)
    first = iota((half, PATCH), 0) == 0
    out = []
    for q in range(Q):
        top = slice(q * PATCH, q * PATCH + half)
        low = slice(q * PATCH + half, (q + 1) * PATCH)
        joint = lambda e, c: same[e] * later[c] + cross[e] * turned[c]
        low_low = joint(low, low)
        out.append(joint(top, top) + jnp.where(first, 0.0, low_low))
        out.append(jnp.where(first, low_low, joint(top, low) - joint(low, top)))
    return jnp.concatenate(out, axis=0)


def scores(product, back_right, back_left):
    both = mm(jnp.concatenate(halves(product), axis=1), back_right[...])
    wide = side_by_side(both[:, :PATCH] + both[:, PATCH:])
    both = mm(back_left[...], jnp.concatenate(halves(wide), axis=0))
    return both[:PATCH] + both[PATCH:]


def signed_lag(shape, dim):
    lag = iota(shape, dim)
    return jnp.where(lag < PATCH // 2, lag, lag - PATCH).astype(f32)


def hat(offset):
    return jnp.maximum(0.0, 1.0 - jnp.abs(offset))


def thirds(value):
    high = value.astype(bf16)
    rest = value - high.astype(f32)
    middle = rest.astype(bf16)
    return high, middle, (rest - middle.astype(f32)).astype(bf16)


def moved(value, selection):
    count = value.shape[0]
    parts = mm(jnp.concatenate(thirds(value), axis=0), selection)
    return parts[:count] + parts[count : 2 * count] + parts[2 * count :]


def kernel(
    sizes,
    images, boundary, anchor, *rest,
):
    n_gz, n_ty, n_tx = sizes
    tables_in, rest = rest[:9], rest[9:]
    (
        mesh_out, drift_out,
        own, before, after, spectra, ties, patch_in, patch_out, sums, land_in, land_out,
        rate, pull, mesh_a, mesh_b,
    ) = rest[:16]
    tables_here, rest = rest[16:25], rest[25:]
    (
        table_sem, own_sem, before_sem, after_sem, up_sem, down_sem, tie_sem, tie_sent,
        patch_sem, patch_sent, land_sem, land_sent, rounds,
    ) = rest
    left, right, right_pair, back_right, back_left, take, spread_cols, spread_rows, give = tables_here
    g, y, x = lax.axis_index("gz"), lax.axis_index("ty"), lax.axis_index("tx")

    def inside(dy, dx):
        ok = None
        for pos, step, count in ((y, dy, n_ty), (x, dx, n_tx)):
            if step:
                here = (pos + step >= 0) & (pos + step < count)
                ok = here if ok is None else ok & here
        return (g >= 0) if ok is None else ok

    def told(semaphore, ok, device):
        @pl.when(ok)
        def _():
            pl.semaphore_signal(semaphore, inc=1, device_id=device, device_id_type=MESH)

        return jnp.where(ok, 1, 0).astype(jnp.int32)

    def within(step):
        return (g + step >= 0) & (g + step < n_gz)

    near = [(within(dz), (g + dz, y, x)) for dz in (-1, 1)]
    near += [(inside(dy, dx), (g, y + dy, x + dx)) for dy, dx in SIDES]

    barrier = pltpu.get_barrier_semaphore()
    greeted = jnp.int32(0)
    for ok, device in near:
        greeted += told(barrier, ok, device)

    def band(ref, k):
        rows = pl.ds(pl.multiple_of(k // (PER // Q) * PATCH, PATCH), PATCH)
        return ref.at[rows, pl.ds(pl.multiple_of(k % (PER // Q) * WIDTH, WIDTH), WIDTH)]

    table_copies = [
        pltpu.make_async_copy(src, dst, table_sem.at[i])
        for i, (src, dst) in enumerate(zip(tables_in, tables_here))
    ]
    for copy in table_copies[:2]:
        copy.start()
    for r in range(PIECES):
        pltpu.make_async_copy(band(images.at[0], r), own.at[r], own_sem.at[r]).start()
    for copy in table_copies[2:]:
        copy.start()
    tie_own = pltpu.make_async_copy(
        anchor.at[0], ties.at[1, pl.ds(SWEEPS, NODES), :], tie_sem.at[slot(0, 0)]
    )
    tie_own.start()
    for r in range(PIECES):

        @pl.when(g == 0)
        def _():
            pltpu.make_async_copy(band(boundary, r), before.at[r], before_sem.at[r]).start()

        @pl.when(g == n_gz - 1)
        def _():
            pltpu.make_async_copy(band(boundary, r), after.at[r], after_sem.at[r]).start()

    pl.semaphore_wait(barrier, greeted)

    def remote(src, dst, sent, arrived, device):
        return pltpu.make_async_remote_copy(
            src_ref=src, dst_ref=dst, send_sem=sent, recv_sem=arrived, device_id=device, device_id_type=MESH
        )

    def to_later(r):
        return remote(band(images.at[0], r), before.at[r], up_sem.at[r], before_sem.at[r], (g + 1, y, x))

    def to_earlier(r):
        return remote(band(images.at[0], r), after.at[r], down_sem.at[r], after_sem.at[r], (g - 1, y, x))

    for r in range(PIECES):

        @pl.when(g < n_gz - 1)
        def _():
            to_later(r).start()

        @pl.when(g > 0)
        def _():
            to_earlier(r).start()

    rows_of = {-1: (0, SWEEPS), 0: (0, NODES), 1: (NODES - SWEEPS, SWEEPS)}
    place_of = {-1: 0, 0: SWEEPS, 1: SWEEPS + NODES}

    def tie_copy(dy, dx):
        first, count = rows_of[dy]
        to = slot(-dy, -dx)
        return remote(
            anchor.at[0, pl.ds(first, count), :],
            ties.at[1 - dx, pl.ds(place_of[-dy], count), :],
            tie_sent.at[to],
            tie_sem.at[to],
            (g, y + dy, x + dx),
        )

    def send_ties(steps):
        for dy, dx in steps:

            @pl.when(inside(dy, dx))
            def _():
                tie_copy(dy, dx).start()

    send_ties(SIDES)
    passed = jnp.int32(0)
    for ok, device in near:
        passed += told(rounds.at[0], ok, device)

    ramp_rows = iota((8, NODES), 1).astype(f32)
    for t in range(n_gz):

        @pl.when(t >= g)
        def _():
            land_in[t] = ramp_rows

    for edge, count, first in ((y == 0, SWEEPS, 0), (y == n_ty - 1, SWEEPS, SWEEPS + NODES)):

        @pl.when(edge)
        def _():
            for d in range(3):
                ties[d, pl.ds(first, count), :] = jnp.zeros((count, NODES), f32)

    for edge, d in ((x == 0, 0), (x == n_tx - 1, 2)):

        @pl.when(edge)
        def _():
            ties[d] = jnp.zeros((WIDE, NODES), f32)

    for dy, dx in AROUND:
        if (dy, dx) != (0, 0):

            @pl.when(jnp.logical_not(inside(dy, dx)))
            def _():
                patch_in[slot(dy, dx)] = jnp.zeros((8, NODES), f32)

        @pl.when(jnp.logical_not(inside(dy, dx)) | (g < 2))
        def _():
            patch_in[9 + slot(dy, dx)] = jnp.zeros((8, NODES), f32)

    def arrival(ref, sem):
        pltpu.make_async_copy(ref, ref, sem).wait()

    for copy in table_copies[:2]:
        copy.wait()

    def own_step(r, carry):
        arrival(own.at[r], own_sem.at[r])
        spectra[r] = packed_spectrum(own[r], left, right)
        return carry

    lax.fori_loop(0, PIECES // 2, own_step, 0)
    pl.semaphore_wait(rounds.at[0], passed)
    send_ties(CORNERS)
    passed_on = jnp.int32(0)
    for step in (-2, -1, 1, 2):
        passed_on += told(rounds.at[1], within(step), (g + step, y, x))
    lax.fori_loop(PIECES // 2, PIECES, own_step, 0)
    pl.semaphore_wait(rounds.at[1], passed_on)
    told(rounds.at[2], within(-4), (g - 4, y, x))

    for copy in table_copies[2:]:
        copy.wait()

    lag_rows = signed_lag((PATCH, PATCH), 0)

    def softmax_sums(wide, k):
        parts = [wide[:, i * PATCH : (i + 1) * PATCH] for i in range(2 * Q)]
        highest = jnp.concatenate([jnp.max(score, axis=0, keepdims=True) for score in parts], axis=0)
        highest = jnp.max(highest, axis=1, keepdims=True)
        for i, score in enumerate(parts):
            pair, q = i // Q, i % Q
            weight = jnp.exp2(score - highest[i : i + 1])
            at = pl.ds((k % (PER // Q) * Q + q) * PER + k // (PER // Q), 1)
            sums[pair, 0, at, :] = jnp.sum(weight, axis=0, keepdims=True)
            sums[pair, 1, at, :] = jnp.sum(weight * lag_rows, axis=0, keepdims=True)

    def band_step(k, carry):
        arrival(before.at[k], before_sem.at[k])
        arrival(after.at[k], after_sem.at[k])
        pair = paired_spectrum(before[k], left, right_pair)
        there = packed_spectrum(after[k], left, right)
        products = [cross_spectrum(pair, spectra[k]), cross_spectrum(pair, there)]
        softmax_sums(scores(jnp.concatenate(products, axis=0), back_right, back_left), k)
        return carry

    lax.fori_loop(0, PIECES, band_step, 0)

    lag_lanes = signed_lag((PER * PER, PATCH), 1)
    col_of = iota((PER * PER, 128), 1) - iota((PER * PER, 128), 0) // PER

    def flow(pair):
        weight = sums[pair, 0]
        scale = (1.0 / STRIDE) / jnp.sum(weight, axis=1, keepdims=True)
        rows = jnp.sum(sums[pair, 1], axis=1, keepdims=True) * scale
        cols = jnp.sum(weight * lag_lanes, axis=1, keepdims=True) * scale
        return rows, cols

    def patch_tile(rows, cols):
        part = jnp.where(col_of == 0, rows, jnp.where(col_of == PER, cols, 0.0))
        part = part[:8] + part[8:]
        return part + pltpu.roll(part, 4, 0)

    nearer, farther = flow(0), flow(1)
    near_scale = jnp.where(g >= 2, 0.5, 1.0).astype(f32)
    for kind, flows in ((1, [0.5 * (b - a) for a, b in zip(nearer, farther)]), (0, [near_scale * v for v in nearer])):
        tile = patch_tile(*flows)
        for d in range(3):
            value = tile if d == 0 else pltpu.roll(tile, 8 * d, 1)
            patch_out[kind, d] = value
            if (kind, d) == (0, 1):
                patch_in[slot(0, 0)] = value

    def patch_copy(kind, dy, dx):
        to = 9 * kind + slot(-dy, -dx)
        return remote(
            patch_out.at[kind, 1 - dx], patch_in.at[to], patch_sent.at[to], patch_sem.at[to],
            (g + kind, y + dy, x + dx),
        )

    ahead = (g >= 1) & (g < n_gz - 1)
    for dy, dx in sorted(AROUND, key=lambda d: -abs(d[0]) - abs(d[1])):

        @pl.when(inside(dy, dx) & ahead)
        def _():
            patch_copy(1, dy, dx).start()

        if (dy, dx) != (0, 0):

            @pl.when(inside(dy, dx))
            def _():
                patch_copy(0, dy, dx).start()

    tie_own.wait()
    for dy, dx in AROUND:
        if (dy, dx) != (0, 0):
            first, count = rows_of[-dy]
            part = ties.at[dx + 1, pl.ds(place_of[dy], count), :]

            @pl.when(inside(dy, dx))
            def _():
                arrival(part, tie_sem.at[slot(dy, dx)])

    lane8, sub8 = iota((8, 128), 1), iota((8, 128), 0)

    def limits(pos, count):
        return jnp.where(pos == 0, 0, -SWEEPS), jnp.where(pos == count - 1, NODES, NODES + SWEEPS)

    row_first, row_last = limits(y, n_ty)
    col_first, col_last = limits(x, n_tx)
    picked = []
    for group in range(GROUPS):
        at = pl.ds(group, 8, stride=GROUPS)
        picked.append(jnp.concatenate([ties[1, at, :], jnp.where(lane8 < 64, ties[2, at, :], ties[0, at, :])], axis=1))
    tie = moved(jnp.concatenate(picked, axis=0), take[...])
    for group in range(GROUPS):
        i = sub8 * GROUPS + (group - SWEEPS)
        for u in range(3):
            j = lane8 % 64 * 3 + (u - SWEEPS)
            kept = (i >= row_first) & (i < row_last) & (j >= col_first) & (j < col_last)
            value = tie[group * 8 : (group + 1) * 8, u * 128 : (u + 1) * 128]
            held = jnp.where(kept, 1.0 / (4.0 + value), 0.0)
            rate[group, :, u * 128 : (u + 1) * 128] = held
            pull[group, :, u * 128 : (u + 1) * 128] = value * held

    @pl.when(within(4))
    def _():
        pl.semaphore_wait(rounds.at[2], 1)

    for dy, dx in AROUND:

        @pl.when(inside(dy, dx) & (g >= 2))
        def _():
            arrival(patch_in.at[9 + slot(dy, dx)], patch_sem.at[9 + slot(dy, dx)])

        if (dy, dx) != (0, 0):

            @pl.when(inside(dy, dx))
            def _():
                arrival(patch_in.at[slot(dy, dx)], patch_sem.at[slot(dy, dx)])

    bands = []
    for dy in (-1, 0, 1):
        total = None
        for dx in (-1, 0, 1):
            tile = patch_in[slot(dy, dx)] + patch_in[9 + slot(dy, dx)]
            total = tile if total is None else total + tile
        bands.append(total)
    bands.append(jnp.zeros((8, 128), f32))
    high, middle, low = (v.astype(f32) for v in thirds(jnp.concatenate(bands, axis=0)))
    patches = (high + pltpu.roll(middle, 32, 1)) + pltpu.roll(low, 64, 1)
    parts = thirds(mm(patches.astype(bf16), spread_cols[...]))
    target = mm(spread_rows[...], jnp.concatenate([*parts, jnp.zeros_like(parts[0])], axis=0))
    for group in range(GROUPS):
        value = target[group * 8 : (group + 1) * 8]
        mesh_a[group] = value
        pull[group] = pull[group] * value

    def sweep(src, dst):
        for group in range(GROUPS):
            here = src[group]
            above = pltpu.roll(src[GROUPS - 1], 1, 0) if group == 0 else src[group - 1]
            below = pltpu.roll(src[0], 7, 0) if group == GROUPS - 1 else src[group + 1]
            first, second, third = (here[:, u * 128 : (u + 1) * 128] for u in range(3))
            beside = jnp.concatenate(
                [pltpu.roll(third, 1, 1) + second, first + third, second + pltpu.roll(first, 127, 1)], axis=1
            )
            dst[group] = ((above + below) + beside) * rate[group] + pull[group]

    def two_sweeps(_, carry):
        sweep(mesh_a, mesh_b)
        sweep(mesh_b, mesh_a)
        return carry

    lax.fori_loop(0, SWEEPS // 2, two_sweeps, 0)

    down, across = jnp.zeros((8, 128), f32), [jnp.zeros((8, 128), f32)] * 3
    for group in range(GROUPS):
        i = sub8 * GROUPS + (group - SWEEPS)
        row_inside = (i >= 0) & (i < NODES)
        row = jnp.zeros((8, 128), f32)
        for u in range(3):
            j = lane8 % 64 * 3 + (u - SWEEPS)
            value = mesh_a[group, :, u * 128 : (u + 1) * 128]
            row += jnp.where((lane8 < 64) & (j >= 0) & (j < NODES), value, 0.0)
            across[u] += jnp.where(row_inside, value, 0.0)
        down += jnp.where(lane8 == i, jnp.sum(row, axis=1, keepdims=True), 0.0)
    across = moved(jnp.concatenate(across, axis=1), give[:, NODES:])
    sub_f, lane_f = (iota((NODES, NODES), d).astype(f32) for d in (0, 1))
    ramp = lane_f[:1]
    own_rows = [
        jnp.clip(ramp + jnp.sum(value, axis=0, keepdims=True) / NODES, 0.0, NODES - 1.0)
        for value in (down, across)
    ]
    land_out[...] = jnp.where(sub8 == 0, own_rows[0], jnp.where(sub8 == 1, own_rows[1], 0.0))

    def land_copy(step):
        return remote(
            land_out, land_in.at[g], land_sent.at[step - 1], land_sem.at[g], (g + step, y, x)
        )

    for step in range(n_gz - 1, 0, -1):

        @pl.when(g + step < n_gz)
        def _():
            land_copy(step).start()

    natural = ties
    ordered = moved(jnp.concatenate([mesh_a[group] for group in range(GROUPS)], axis=0), give[...])
    for group in range(GROUPS):
        at = pl.ds(group, 8, stride=GROUPS)
        for c in range(2):
            natural[c, at, :] = ordered[group * 8 : (group + 1) * 8, c * NODES : (c + 1) * NODES]
    for c in range(2):
        mesh_out[0, c] = natural[c, SWEEPS : SWEEPS + NODES, :]

    for r in range(PIECES):

        @pl.when(g < n_gz - 1)
        def _():
            to_later(r).wait_send()

        @pl.when(g > 0)
        def _():
            to_earlier(r).wait_send()

    for dy, dx in AROUND:
        if (dy, dx) != (0, 0):

            @pl.when(inside(dy, dx))
            def _():
                tie_copy(dy, dx).wait_send()
                patch_copy(0, dy, dx).wait_send()

        @pl.when(inside(dy, dx) & ahead)
        def _():
            patch_copy(1, dy, dx).wait_send()

    eye = sub_f == lane_f
    to_row = lambda col: jnp.sum(jnp.where(eye, col, 0.0), axis=0, keepdims=True)
    to_col = lambda row: jnp.sum(jnp.where(eye, row, 0.0), axis=1, keepdims=True)
    placed = [to_col(row) for row in own_rows]
    for t in range(n_gz - 2, -1, -1):

        @pl.when(t < g)
        def _():
            arrival(land_in.at[t], land_sem.at[t])

        for c in range(2):
            landing = land_in[t, c : c + 1, :]
            if (n_gz - 2 - t) % 2 == 0:
                placed[c] = jnp.sum(hat(landing - sub_f) * placed[c], axis=0, keepdims=True)
            else:
                placed[c] = jnp.sum(hat(to_col(landing) - lane_f) * placed[c], axis=1, keepdims=True)
    for c in range(2):
        value = to_row(placed[c]) if n_gz % 2 else placed[c]
        drift_out[0, 0, 0, c : c + 1, :] = value - ramp

    for step in range(1, n_gz):

        @pl.when(g + step < n_gz)
        def _():
            land_copy(step).wait_send()


def finish(mesh_in, drift_in, mesh_out, drift_out, sems):
    copies = [
        pltpu.make_async_copy(src, dst, sems.at[i])
        for i, (src, dst) in enumerate(((mesh_in, mesh_out), (drift_in, drift_out)))
    ]
    for copy in copies:
        copy.start()
    for copy in copies:
        copy.wait()


def solution(mesh):
    sizes = tuple(mesh.shape[name] for name in ("gz", "ty", "tx"))
    n_gz = sizes[0]
    constants = tables()
    dma = pltpu.SemaphoreType.DMA
    vmem = pl.BlockSpec(memory_space=pltpu.VMEM)
    hbm = pl.BlockSpec(memory_space=pltpu.HBM)

    def local(images, boundary, anchor):
        results = (
            jax.ShapeDtypeStruct((1, 2, NODES, NODES), f32),
            jax.ShapeDtypeStruct((1, 1, 1, 2, NODES), f32),
        )
        found = pl.pallas_call(
            functools.partial(kernel, sizes),
            out_shape=results,
            in_specs=[hbm] * (3 + len(constants)),
            out_specs=(vmem, vmem),
            scratch_shapes=[
                pltpu.VMEM((PIECES, PATCH, WIDTH), bf16),
                pltpu.VMEM((PIECES, PATCH, WIDTH), bf16),
                pltpu.VMEM((PIECES, PATCH, WIDTH), bf16),
                pltpu.VMEM((PIECES, WIDTH, PATCH), f32),
                pltpu.VMEM((3, WIDE, NODES), f32),
                pltpu.VMEM((18, 8, NODES), f32),
                pltpu.VMEM((2, 3, 8, NODES), f32),
                pltpu.VMEM((2, 2, PER * PER, PATCH), f32),
                pltpu.VMEM((n_gz, 8, NODES), f32),
                pltpu.VMEM((8, NODES), f32),
                pltpu.VMEM((GROUPS, 8, LANES), f32),
                pltpu.VMEM((GROUPS, 8, LANES), f32),
                pltpu.VMEM((GROUPS, 8, LANES), f32),
                pltpu.VMEM((GROUPS, 8, LANES), f32),
                *(pltpu.VMEM(c.shape, bf16) for c in constants),
                dma((len(constants),)),
                dma((PIECES,)),
                dma((PIECES,)),
                dma((PIECES,)),
                dma((PIECES,)),
                dma((PIECES,)),
                dma((9,)),
                dma((9,)),
                dma((18,)),
                dma((18,)),
                dma((n_gz,)),
                dma((n_gz,)),
                pltpu.SemaphoreType.REGULAR((3,)),
            ],
            compiler_params=pltpu.CompilerParams(
                collective_id=0, has_side_effects=True, vmem_limit_bytes=GRANT,
            ),
            name="align",
        )(*(pltpu.with_memory_space_constraint(v, pltpu.HBM) for v in (images, boundary, anchor, *map(jnp.asarray, constants))))
        return pl.pallas_call(
            finish,
            out_shape=results,
            in_specs=[vmem, vmem],
            out_specs=(hbm, hbm),
            scratch_shapes=[dma((2,))],
            compiler_params=pltpu.CompilerParams(vmem_limit_bytes=4 * 1024 * 1024),
            name="finish",
        )(*found)

    return jax.shard_map(
        local,
        mesh=mesh,
        in_specs=(P("gz", "ty", "tx"), P("ty", "tx"), P("gz", "ty", "tx")),
        out_specs=(P("gz", None, "ty", "tx"), P("gz", "ty", "tx", None, None)),
        check_vma=False,
    )
```

```python
import functools
import math

import jax
import jax.numpy as jnp
import numpy as np
from jax import lax
from jax.experimental import pallas as pl
from jax.experimental.pallas import tpu as pltpu
from jax.sharding import PartitionSpec as P

PATCH = 128
STRIDE = 4
SWEEPS = 32
TRIP = 8
TILE = 512
NODES = 128
PER = TILE // PATCH
Q = 4
WIDTH = Q * PATCH
PIECES = PER * PER // Q
WIDE = NODES + 2 * SWEEPS
GROUPS = WIDE // 8
LANES = 2 * WIDE

GRANT = 48 * 1024 * 1024

f32 = jnp.float32
bf16 = jnp.bfloat16
MESH = pl.DeviceIdType.MESH
AROUND = [(dy, dx) for dy in (-1, 0, 1) for dx in (-1, 0, 1)]
SIDES = [(-1, 0), (1, 0), (0, -1), (0, 1)]
CORNERS = [(-1, -1), (-1, 1), (1, -1), (1, 1)]


def slot(dy, dx):
    return (dy + 1) * 3 + dx + 1


def pieces(table, count):
    parts = []
    rest = np.asarray(table, np.float64)
    for _ in range(count):
        part = rest.astype(jnp.bfloat16)
        parts.append(part)
        rest = rest - part.astype(np.float64)
    return parts


def spread_table():
    pos = (np.arange(NODES) + 0.5) * STRIDE / PATCH - 0.5
    weights = np.maximum(0.0, 1.0 - np.abs(pos[:, None] - np.arange(PER)[None, :]))
    return weights / weights.sum(axis=1, keepdims=True)


def tables():
    half = PATCH // 2
    n = np.arange(PATCH)
    angle = lambda k: 2.0 * np.pi * (n[:, None] * k[None, :] % PATCH) / PATCH
    low, high = np.arange(half), np.arange(1, half)
    cos_low, sin_high = np.cos(angle(low)), np.sin(angle(high))
    last = np.cos(np.pi * n)[:, None]
    zero = np.zeros_like(last)
    basis = np.concatenate([cos_low, last, sin_high], axis=1)
    same = np.concatenate([cos_low, last, cos_low[:, 1:]], axis=1)
    cross = np.concatenate([zero, sin_high, zero, -sin_high], axis=1)
    weight = np.full(PATCH, 2.0 / PATCH)
    weight[[0, half]] = 1.0 / PATCH
    inverse = basis * weight[None, :]

    b_hi, b_lo = pieces(basis, 2)
    s_hi, s_lo = pieces(same, 2)
    c_hi, c_lo = pieces(cross, 2)
    r_hi, r_lo = pieces(inverse.T, 2)
    l_hi, l_lo = pieces(inverse * (math.log2(math.e) / PATCH), 2)
    left = np.concatenate([b_hi.T, b_lo.T], axis=0)
    right = np.concatenate([b_hi, b_lo], axis=1)
    right_pair = np.concatenate([s_hi, c_hi, s_lo, c_lo], axis=1)
    back_right = np.concatenate([r_hi, r_lo], axis=1)
    back_left = np.concatenate([l_hi, l_lo], axis=0)
    twice = lambda t, axis: np.concatenate([t, t], axis=axis)

    spread = spread_table()
    rows = np.zeros((WIDE, 128))
    for group in range(GROUPS):
        for sub in range(8):
            i = sub * GROUPS + group - SWEEPS
            dy = i // NODES
            for piece in range(3):
                first = piece * 32 + (dy + 1) * 8
                rows[group * 8 + sub, first : first + PER] = spread[i - dy * NODES]
    cols = np.zeros((128, LANES))
    take = np.zeros((256, LANES))
    give = np.zeros((LANES, 2 * NODES))
    for u in range(3):
        for lane in range(128):
            comp, j = lane // 64, lane % 64 * 3 + u - SWEEPS
            dx = j // NODES
            at = u * 128 + lane
            for piece in range(3):
                first = piece * 32 + (dx + 1) * 8 + comp * PER
                cols[first : first + PER, at] = spread[j - dx * NODES]
            take[j if dx == 0 else 128 + j % NODES, at] = 1.0
            if dx == 0:
                give[at, comp * NODES + j] = 1.0
    return tuple(
        t.astype(jnp.bfloat16)
        for t in (
            left,
            twice(right, 0),
            twice(right_pair, 0),
            twice(back_right, 0),
            twice(back_left, 1),
            take,
            cols,
            rows,
            give,
        )
    )


def mm(a, b):
    return jnp.dot(a, b, preferred_element_type=f32)


def halves(value):
    hi = value.astype(bf16)
    return hi, (value - hi.astype(f32)).astype(bf16)


def iota(shape, dim):
    return lax.broadcasted_iota(jnp.int32, shape, dim)


def stacked_rows(wide):
    return jnp.concatenate([wide[:, q * PATCH : (q + 1) * PATCH] for q in range(wide.shape[1] // PATCH)], axis=0)


def side_by_side(tall):
    return jnp.concatenate([tall[q * PATCH : (q + 1) * PATCH] for q in range(tall.shape[0] // PATCH)], axis=1)


def row_pass(pixels, left):
    both = mm(left[...], pixels)
    return jnp.concatenate(halves(stacked_rows(both[:PATCH] + both[PATCH:])), axis=1)


def packed_spectrum(pixels, left, right):
    both = mm(row_pass(pixels, left), right[...])
    return both[:, :PATCH] + both[:, PATCH:]


def paired_spectrum(pixels, left, right_pair):
    both = mm(row_pass(pixels, left), right_pair[...])
    return (
        both[:, :PATCH] + both[:, 2 * PATCH : 3 * PATCH],
        both[:, PATCH : 2 * PATCH] + both[:, 3 * PATCH :],
    )


def cross_spectrum(pair, later):
    half = PATCH // 2
    same, cross = pair
    turned = pltpu.roll(later, half, 1)
    first = iota((half, PATCH), 0) == 0
    out = []
    for q in range(Q):
        top = slice(q * PATCH, q * PATCH + half)
        low = slice(q * PATCH + half, (q + 1) * PATCH)
        joint = lambda e, c: same[e] * later[c] + cross[e] * turned[c]
        low_low = joint(low, low)
        out.append(joint(top, top) + jnp.where(first, 0.0, low_low))
        out.append(jnp.where(first, low_low, joint(top, low) - joint(low, top)))
    return jnp.concatenate(out, axis=0)


def scores(product, back_right, back_left):
    both = mm(jnp.concatenate(halves(product), axis=1), back_right[...])
    wide = side_by_side(both[:, :PATCH] + both[:, PATCH:])
    both = mm(back_left[...], jnp.concatenate(halves(wide), axis=0))
    return both[:PATCH] + both[PATCH:]


def signed_lag(shape, dim):
    lag = iota(shape, dim)
    return jnp.where(lag < PATCH // 2, lag, lag - PATCH).astype(f32)


def hat(offset):
    return jnp.maximum(0.0, 1.0 - jnp.abs(offset))


def thirds(value):
    high = value.astype(bf16)
    rest = value - high.astype(f32)
    middle = rest.astype(bf16)
    return high, middle, (rest - middle.astype(f32)).astype(bf16)


def moved(value, selection):
    count = value.shape[0]
    parts = mm(jnp.concatenate(thirds(value), axis=0), selection)
    return parts[:count] + parts[count : 2 * count] + parts[2 * count :]


def kernel(
    sizes,
    images, boundary, anchor, *rest,
):
    n_gz, n_ty, n_tx = sizes
    tables_in, rest = rest[:9], rest[9:]
    (
        mesh_out, drift_out,
        own, before, after, spectra, ties, patch_in, patch_out, sums, land_in, land_out,
        rate, pull, mesh_a, mesh_b,
    ) = rest[:16]
    tables_here, rest = rest[16:25], rest[25:]
    (
        table_sem, own_sem, before_sem, after_sem, up_sem, down_sem, tie_sem, tie_sent,
        patch_sem, patch_sent, land_sem, land_sent, rounds,
    ) = rest
    left, right, right_pair, back_right, back_left, take, spread_cols, spread_rows, give = tables_here
    g, y, x = lax.axis_index("gz"), lax.axis_index("ty"), lax.axis_index("tx")

    def inside(dy, dx):
        ok = None
        for pos, step, count in ((y, dy, n_ty), (x, dx, n_tx)):
            if step:
                here = (pos + step >= 0) & (pos + step < count)
                ok = here if ok is None else ok & here
        return (g >= 0) if ok is None else ok

    def told(semaphore, ok, device):
        @pl.when(ok)
        def _():
            pl.semaphore_signal(semaphore, inc=1, device_id=device, device_id_type=MESH)

        return jnp.where(ok, 1, 0).astype(jnp.int32)

    def within(step):
        return (g + step >= 0) & (g + step < n_gz)

    near = [(within(dz), (g + dz, y, x)) for dz in (-1, 1)]
    near += [(inside(dy, dx), (g, y + dy, x + dx)) for dy, dx in SIDES]

    barrier = pltpu.get_barrier_semaphore()
    greeted = jnp.int32(0)
    for ok, device in near:
        greeted += told(barrier, ok, device)

    def band(ref, k):
        rows = pl.ds(pl.multiple_of(k // (PER // Q) * PATCH, PATCH), PATCH)
        return ref.at[rows, pl.ds(pl.multiple_of(k % (PER // Q) * WIDTH, WIDTH), WIDTH)]

    table_copies = [
        pltpu.make_async_copy(src, dst, table_sem.at[i])
        for i, (src, dst) in enumerate(zip(tables_in, tables_here))
    ]
    for copy in table_copies[:2]:
        copy.start()
    for r in range(PIECES):
        pltpu.make_async_copy(band(images.at[0], r), own.at[r], own_sem.at[r]).start()
    for copy in table_copies[2:]:
        copy.start()
    tie_own = pltpu.make_async_copy(
        anchor.at[0], ties.at[1, pl.ds(SWEEPS, NODES), :], tie_sem.at[slot(0, 0)]
    )
    tie_own.start()
    for r in range(PIECES):

        @pl.when(g == 0)
        def _():
            pltpu.make_async_copy(band(boundary, r), before.at[r], before_sem.at[r]).start()

        @pl.when(g == n_gz - 1)
        def _():
            pltpu.make_async_copy(band(boundary, r), after.at[r], after_sem.at[r]).start()

    pl.semaphore_wait(barrier, greeted)

    def remote(src, dst, sent, arrived, device):
        return pltpu.make_async_remote_copy(
            src_ref=src, dst_ref=dst, send_sem=sent, recv_sem=arrived, device_id=device, device_id_type=MESH
        )

    def to_later(r):
        return remote(own.at[r], before.at[r], up_sem.at[r], before_sem.at[r], (g + 1, y, x))

    def to_earlier(r):
        return remote(own.at[r], after.at[r], down_sem.at[r], after_sem.at[r], (g - 1, y, x))

    for r in range(PIECES):
        pltpu.make_async_copy(own.at[r], own.at[r], own_sem.at[r]).wait()

        @pl.when(g < n_gz - 1)
        def _():
            to_later(r).start()

        @pl.when(g > 0)
        def _():
            to_earlier(r).start()

    rows_of = {-1: (0, SWEEPS), 0: (0, NODES), 1: (NODES - SWEEPS, SWEEPS)}
    place_of = {-1: 0, 0: SWEEPS, 1: SWEEPS + NODES}

    def tie_copy(dy, dx):
        first, count = rows_of[dy]
        to = slot(-dy, -dx)
        return remote(
            anchor.at[0, pl.ds(first, count), :],
            ties.at[1 - dx, pl.ds(place_of[-dy], count), :],
            tie_sent.at[to],
            tie_sem.at[to],
            (g, y + dy, x + dx),
        )

    def send_ties(steps):
        for dy, dx in steps:

            @pl.when(inside(dy, dx))
            def _():
                tie_copy(dy, dx).start()

    send_ties(SIDES)
    passed = jnp.int32(0)
    for ok, device in near:
        passed += told(rounds.at[0], ok, device)

    ramp_rows = iota((8, NODES), 1).astype(f32)
    for t in range(n_gz):

        @pl.when(t >= g)
        def _():
            land_in[t] = ramp_rows

    for edge, count, first in ((y == 0, SWEEPS, 0), (y == n_ty - 1, SWEEPS, SWEEPS + NODES)):

        @pl.when(edge)
        def _():
            for d in range(3):
                ties[d, pl.ds(first, count), :] = jnp.zeros((count, NODES), f32)

    for edge, d in ((x == 0, 0), (x == n_tx - 1, 2)):

        @pl.when(edge)
        def _():
            ties[d] = jnp.zeros((WIDE, NODES), f32)

    for dy, dx in AROUND:
        if (dy, dx) != (0, 0):

            @pl.when(jnp.logical_not(inside(dy, dx)))
            def _():
                patch_in[slot(dy, dx)] = jnp.zeros((8, NODES), f32)

        @pl.when(jnp.logical_not(inside(dy, dx)) | (g < 2))
        def _():
            patch_in[9 + slot(dy, dx)] = jnp.zeros((8, NODES), f32)

    def arrival(ref, sem):
        pltpu.make_async_copy(ref, ref, sem).wait()

    for copy in table_copies[:2]:
        copy.wait()

    def own_step(r, carry):
        spectra[r] = packed_spectrum(own[r], left, right)
        return carry

    lax.fori_loop(0, PIECES // 2, own_step, 0)
    pl.semaphore_wait(rounds.at[0], passed)
    send_ties(CORNERS)
    passed_on = jnp.int32(0)
    for step in (-2, -1, 1, 2):
        passed_on += told(rounds.at[1], within(step), (g + step, y, x))
    lax.fori_loop(PIECES // 2, PIECES, own_step, 0)
    pl.semaphore_wait(rounds.at[1], passed_on)
    told(rounds.at[2], within(-4), (g - 4, y, x))

    for copy in table_copies[2:]:
        copy.wait()

    lag_rows = signed_lag((PATCH, PATCH), 0)

    def softmax_sums(wide, k):
        parts = [wide[:, i * PATCH : (i + 1) * PATCH] for i in range(2 * Q)]
        highest = jnp.concatenate([jnp.max(score, axis=0, keepdims=True) for score in parts], axis=0)
        highest = jnp.max(highest, axis=1, keepdims=True)
        for i, score in enumerate(parts):
            pair, q = i // Q, i % Q
            weight = jnp.exp2(score - highest[i : i + 1])
            at = pl.ds((k % (PER // Q) * Q + q) * PER + k // (PER // Q), 1)
            sums[pair, 0, at, :] = jnp.sum(weight, axis=0, keepdims=True)
            sums[pair, 1, at, :] = jnp.sum(weight * lag_rows, axis=0, keepdims=True)

    def band_step(k, carry):
        arrival(before.at[k], before_sem.at[k])
        arrival(after.at[k], after_sem.at[k])
        pair = paired_spectrum(before[k], left, right_pair)
        there = packed_spectrum(after[k], left, right)
        products = [cross_spectrum(pair, spectra[k]), cross_spectrum(pair, there)]
        softmax_sums(scores(jnp.concatenate(products, axis=0), back_right, back_left), k)
        return carry

    lax.fori_loop(0, PIECES, band_step, 0)

    lag_lanes = signed_lag((PER * PER, PATCH), 1)
    col_of = iota((PER * PER, 128), 1) - iota((PER * PER, 128), 0) // PER

    def flow(pair):
        weight = sums[pair, 0]
        scale = (1.0 / STRIDE) / jnp.sum(weight, axis=1, keepdims=True)
        rows = jnp.sum(sums[pair, 1], axis=1, keepdims=True) * scale
        cols = jnp.sum(weight * lag_lanes, axis=1, keepdims=True) * scale
        return rows, cols

    def patch_tile(rows, cols):
        part = jnp.where(col_of == 0, rows, jnp.where(col_of == PER, cols, 0.0))
        part = part[:8] + part[8:]
        return part + pltpu.roll(part, 4, 0)

    nearer, farther = flow(0), flow(1)
    near_scale = jnp.where(g >= 2, 0.5, 1.0).astype(f32)
    for kind, flows in ((1, [0.5 * (b - a) for a, b in zip(nearer, farther)]), (0, [near_scale * v for v in nearer])):
        tile = patch_tile(*flows)
        for d in range(3):
            value = tile if d == 0 else pltpu.roll(tile, 8 * d, 1)
            patch_out[kind, d] = value
            if (kind, d) == (0, 1):
                patch_in[slot(0, 0)] = value

    def patch_copy(kind, dy, dx):
        to = 9 * kind + slot(-dy, -dx)
        return remote(
            patch_out.at[kind, 1 - dx], patch_in.at[to], patch_sent.at[to], patch_sem.at[to],
            (g + kind, y + dy, x + dx),
        )

    ahead = (g >= 1) & (g < n_gz - 1)
    for dy, dx in sorted(AROUND, key=lambda d: -abs(d[0]) - abs(d[1])):

        @pl.when(inside(dy, dx) & ahead)
        def _():
            patch_copy(1, dy, dx).start()

        if (dy, dx) != (0, 0):

            @pl.when(inside(dy, dx))
            def _():
                patch_copy(0, dy, dx).start()

    tie_own.wait()
    for dy, dx in AROUND:
        if (dy, dx) != (0, 0):
            first, count = rows_of[-dy]
            part = ties.at[dx + 1, pl.ds(place_of[dy], count), :]

            @pl.when(inside(dy, dx))
            def _():
                arrival(part, tie_sem.at[slot(dy, dx)])

    lane8, sub8 = iota((8, 128), 1), iota((8, 128), 0)

    def limits(pos, count):
        return jnp.where(pos == 0, 0, -SWEEPS), jnp.where(pos == count - 1, NODES, NODES + SWEEPS)

    row_first, row_last = limits(y, n_ty)
    col_first, col_last = limits(x, n_tx)
    picked = []
    for group in range(GROUPS):
        at = pl.ds(group, 8, stride=GROUPS)
        picked.append(jnp.concatenate([ties[1, at, :], jnp.where(lane8 < 64, ties[2, at, :], ties[0, at, :])], axis=1))
    tie = moved(jnp.concatenate(picked, axis=0), take[...])
    for group in range(GROUPS):
        i = sub8 * GROUPS + (group - SWEEPS)
        for u in range(3):
            j = lane8 % 64 * 3 + (u - SWEEPS)
            kept = (i >= row_first) & (i < row_last) & (j >= col_first) & (j < col_last)
            value = tie[group * 8 : (group + 1) * 8, u * 128 : (u + 1) * 128]
            held = jnp.where(kept, 1.0 / (4.0 + value), 0.0)
            rate[group, :, u * 128 : (u + 1) * 128] = held
            pull[group, :, u * 128 : (u + 1) * 128] = value * held

    @pl.when(within(4))
    def _():
        pl.semaphore_wait(rounds.at[2], 1)

    for dy, dx in AROUND:

        @pl.when(inside(dy, dx) & (g >= 2))
        def _():
            arrival(patch_in.at[9 + slot(dy, dx)], patch_sem.at[9 + slot(dy, dx)])

        if (dy, dx) != (0, 0):

            @pl.when(inside(dy, dx))
            def _():
                arrival(patch_in.at[slot(dy, dx)], patch_sem.at[slot(dy, dx)])

    bands = []
    for dy in (-1, 0, 1):
        total = None
        for dx in (-1, 0, 1):
            tile = patch_in[slot(dy, dx)] + patch_in[9 + slot(dy, dx)]
            total = tile if total is None else total + tile
        bands.append(total)
    bands.append(jnp.zeros((8, 128), f32))
    high, middle, low = (v.astype(f32) for v in thirds(jnp.concatenate(bands, axis=0)))
    patches = (high + pltpu.roll(middle, 32, 1)) + pltpu.roll(low, 64, 1)
    parts = thirds(mm(patches.astype(bf16), spread_cols[...]))
    target = mm(spread_rows[...], jnp.concatenate([*parts, jnp.zeros_like(parts[0])], axis=0))
    for group in range(GROUPS):
        value = target[group * 8 : (group + 1) * 8]
        mesh_a[group] = value
        pull[group] = pull[group] * value

    def sweep(src, dst):
        for group in range(GROUPS):
            here = src[group]
            above = pltpu.roll(src[GROUPS - 1], 1, 0) if group == 0 else src[group - 1]
            below = pltpu.roll(src[0], 7, 0) if group == GROUPS - 1 else src[group + 1]
            first, second, third = (here[:, u * 128 : (u + 1) * 128] for u in range(3))
            beside = jnp.concatenate(
                [pltpu.roll(third, 1, 1) + second, first + third, second + pltpu.roll(first, 127, 1)], axis=1
            )
            dst[group] = ((above + below) + beside) * rate[group] + pull[group]

    def some_sweeps(_, carry):
        for _ in range(TRIP // 2):
            sweep(mesh_a, mesh_b)
            sweep(mesh_b, mesh_a)
        return carry

    lax.fori_loop(0, SWEEPS // TRIP, some_sweeps, 0)

    down, across = jnp.zeros((8, 128), f32), [jnp.zeros((8, 128), f32)] * 3
    for group in range(GROUPS):
        i = sub8 * GROUPS + (group - SWEEPS)
        row_inside = (i >= 0) & (i < NODES)
        row = jnp.zeros((8, 128), f32)
        for u in range(3):
            j = lane8 % 64 * 3 + (u - SWEEPS)
            value = mesh_a[group, :, u * 128 : (u + 1) * 128]
            row += jnp.where((lane8 < 64) & (j >= 0) & (j < NODES), value, 0.0)
            across[u] += jnp.where(row_inside, value, 0.0)
        down += jnp.where(lane8 == i, jnp.sum(row, axis=1, keepdims=True), 0.0)
    across = moved(jnp.concatenate(across, axis=1), give[:, NODES:])
    sub_f, lane_f = (iota((NODES, NODES), d).astype(f32) for d in (0, 1))
    ramp = lane_f[:1]
    own_rows = [
        jnp.clip(ramp + jnp.sum(value, axis=0, keepdims=True) / NODES, 0.0, NODES - 1.0)
        for value in (down, across)
    ]
    land_out[...] = jnp.where(sub8 == 0, own_rows[0], jnp.where(sub8 == 1, own_rows[1], 0.0))

    def land_copy(step):
        return remote(
            land_out, land_in.at[g], land_sent.at[step - 1], land_sem.at[g], (g + step, y, x)
        )

    for step in range(n_gz - 1, 0, -1):

        @pl.when(g + step < n_gz)
        def _():
            land_copy(step).start()

    natural = ties
    ordered = moved(jnp.concatenate([mesh_a[group] for group in range(GROUPS)], axis=0), give[...])
    for group in range(GROUPS):
        at = pl.ds(group, 8, stride=GROUPS)
        for c in range(2):
            natural[c, at, :] = ordered[group * 8 : (group + 1) * 8, c * NODES : (c + 1) * NODES]
    for c in range(2):
        mesh_out[0, c] = natural[c, SWEEPS : SWEEPS + NODES, :]

    for r in range(PIECES):

        @pl.when(g < n_gz - 1)
        def _():
            to_later(r).wait_send()

        @pl.when(g > 0)
        def _():
            to_earlier(r).wait_send()

    for dy, dx in AROUND:
        if (dy, dx) != (0, 0):

            @pl.when(inside(dy, dx))
            def _():
                tie_copy(dy, dx).wait_send()
                patch_copy(0, dy, dx).wait_send()

        @pl.when(inside(dy, dx) & ahead)
        def _():
            patch_copy(1, dy, dx).wait_send()

    eye = sub_f == lane_f
    to_row = lambda col: jnp.sum(jnp.where(eye, col, 0.0), axis=0, keepdims=True)
    to_col = lambda row: jnp.sum(jnp.where(eye, row, 0.0), axis=1, keepdims=True)
    placed = [to_col(row) for row in own_rows]
    for t in range(n_gz - 2, -1, -1):

        @pl.when(t < g)
        def _():
            arrival(land_in.at[t], land_sem.at[t])

        for c in range(2):
            landing = land_in[t, c : c + 1, :]
            if (n_gz - 2 - t) % 2 == 0:
                placed[c] = jnp.sum(hat(landing - sub_f) * placed[c], axis=0, keepdims=True)
            else:
                placed[c] = jnp.sum(hat(to_col(landing) - lane_f) * placed[c], axis=1, keepdims=True)
    for c in range(2):
        value = to_row(placed[c]) if n_gz % 2 else placed[c]
        drift_out[0, 0, 0, c : c + 1, :] = value - ramp

    for step in range(1, n_gz):

        @pl.when(g + step < n_gz)
        def _():
            land_copy(step).wait_send()


def finish(mesh_in, drift_in, mesh_out, drift_out, sems):
    copies = [
        pltpu.make_async_copy(src, dst, sems.at[i])
        for i, (src, dst) in enumerate(((mesh_in, mesh_out), (drift_in, drift_out)))
    ]
    for copy in copies:
        copy.start()
    for copy in copies:
        copy.wait()


def solution(mesh):
    sizes = tuple(mesh.shape[name] for name in ("gz", "ty", "tx"))
    n_gz = sizes[0]
    constants = tables()
    dma = pltpu.SemaphoreType.DMA
    vmem = pl.BlockSpec(memory_space=pltpu.VMEM)
    hbm = pl.BlockSpec(memory_space=pltpu.HBM)

    def local(images, boundary, anchor):
        results = (
            jax.ShapeDtypeStruct((1, 2, NODES, NODES), f32),
            jax.ShapeDtypeStruct((1, 1, 1, 2, NODES), f32),
        )
        found = pl.pallas_call(
            functools.partial(kernel, sizes),
            out_shape=results,
            in_specs=[hbm] * (3 + len(constants)),
            out_specs=(vmem, vmem),
            scratch_shapes=[
                pltpu.VMEM((PIECES, PATCH, WIDTH), bf16),
                pltpu.VMEM((PIECES, PATCH, WIDTH), bf16),
                pltpu.VMEM((PIECES, PATCH, WIDTH), bf16),
                pltpu.VMEM((PIECES, WIDTH, PATCH), f32),
                pltpu.VMEM((3, WIDE, NODES), f32),
                pltpu.VMEM((18, 8, NODES), f32),
                pltpu.VMEM((2, 3, 8, NODES), f32),
                pltpu.VMEM((2, 2, PER * PER, PATCH), f32),
                pltpu.VMEM((n_gz, 8, NODES), f32),
                pltpu.VMEM((8, NODES), f32),
                pltpu.VMEM((GROUPS, 8, LANES), f32),
                pltpu.VMEM((GROUPS, 8, LANES), f32),
                pltpu.VMEM((GROUPS, 8, LANES), f32),
                pltpu.VMEM((GROUPS, 8, LANES), f32),
                *(pltpu.VMEM(c.shape, bf16) for c in constants),
                dma((len(constants),)),
                dma((PIECES,)),
                dma((PIECES,)),
                dma((PIECES,)),
                dma((PIECES,)),
                dma((PIECES,)),
                dma((9,)),
                dma((9,)),
                dma((18,)),
                dma((18,)),
                dma((n_gz,)),
                dma((n_gz,)),
                pltpu.SemaphoreType.REGULAR((3,)),
            ],
            compiler_params=pltpu.CompilerParams(
                collective_id=0, has_side_effects=True, vmem_limit_bytes=GRANT,
            ),
            name="align",
        )(*(pltpu.with_memory_space_constraint(v, pltpu.HBM) for v in (images, boundary, anchor, *map(jnp.asarray, constants))))
        return pl.pallas_call(
            finish,
            out_shape=results,
            in_specs=[vmem, vmem],
            out_specs=(hbm, hbm),
            scratch_shapes=[dma((2,))],
            compiler_params=pltpu.CompilerParams(vmem_limit_bytes=4 * 1024 * 1024),
            name="finish",
        )(*found)

    return jax.shard_map(
        local,
        mesh=mesh,
        in_specs=(P("gz", "ty", "tx"), P("ty", "tx"), P("gz", "ty", "tx")),
        out_specs=(P("gz", None, "ty", "tx"), P("gz", "ty", "tx", None, None)),
        check_vma=False,
    )
```

```python
import functools
import math

import jax
import jax.numpy as jnp
import numpy as np
from jax import lax
from jax.experimental import pallas as pl
from jax.experimental.pallas import tpu as pltpu
from jax.sharding import PartitionSpec as P

PATCH = 128
STRIDE = 4
SWEEPS = 32
TRIP = 32
TILE = 512
NODES = 128
PER = TILE // PATCH
Q = 4
WIDTH = Q * PATCH
PIECES = PER * PER // Q
WIDE = NODES + 2 * SWEEPS
GROUPS = WIDE // 8
LANES = 2 * WIDE

GRANT = 48 * 1024 * 1024

f32 = jnp.float32
bf16 = jnp.bfloat16
MESH = pl.DeviceIdType.MESH
AROUND = [(dy, dx) for dy in (-1, 0, 1) for dx in (-1, 0, 1)]
SIDES = [(-1, 0), (1, 0), (0, -1), (0, 1)]
CORNERS = [(-1, -1), (-1, 1), (1, -1), (1, 1)]


def slot(dy, dx):
    return (dy + 1) * 3 + dx + 1


def pieces(table, count):
    parts = []
    rest = np.asarray(table, np.float64)
    for _ in range(count):
        part = rest.astype(jnp.bfloat16)
        parts.append(part)
        rest = rest - part.astype(np.float64)
    return parts


def spread_table():
    pos = (np.arange(NODES) + 0.5) * STRIDE / PATCH - 0.5
    weights = np.maximum(0.0, 1.0 - np.abs(pos[:, None] - np.arange(PER)[None, :]))
    return weights / weights.sum(axis=1, keepdims=True)


def tables():
    half = PATCH // 2
    n = np.arange(PATCH)
    angle = lambda k: 2.0 * np.pi * (n[:, None] * k[None, :] % PATCH) / PATCH
    low, high = np.arange(half), np.arange(1, half)
    cos_low, sin_high = np.cos(angle(low)), np.sin(angle(high))
    last = np.cos(np.pi * n)[:, None]
    zero = np.zeros_like(last)
    basis = np.concatenate([cos_low, last, sin_high], axis=1)
    same = np.concatenate([cos_low, last, cos_low[:, 1:]], axis=1)
    cross = np.concatenate([zero, sin_high, zero, -sin_high], axis=1)
    weight = np.full(PATCH, 2.0 / PATCH)
    weight[[0, half]] = 1.0 / PATCH
    inverse = basis * weight[None, :]

    b_hi, b_lo = pieces(basis, 2)
    s_hi, s_lo = pieces(same, 2)
    c_hi, c_lo = pieces(cross, 2)
    r_hi, r_lo = pieces(inverse.T, 2)
    l_hi, l_lo = pieces(inverse * (math.log2(math.e) / PATCH), 2)
    left = np.concatenate([b_hi.T, b_lo.T], axis=0)
    right = np.concatenate([b_hi, b_lo], axis=1)
    right_pair = np.concatenate([s_hi, c_hi, s_lo, c_lo], axis=1)
    back_right = np.concatenate([r_hi, r_lo], axis=1)
    back_left = np.concatenate([l_hi, l_lo], axis=0)
    twice = lambda t, axis: np.concatenate([t, t], axis=axis)

    spread = spread_table()
    rows = np.zeros((WIDE, 128))
    for group in range(GROUPS):
        for sub in range(8):
            i = sub * GROUPS + group - SWEEPS
            dy = i // NODES
            for piece in range(3):
                first = piece * 32 + (dy + 1) * 8
                rows[group * 8 + sub, first : first + PER] = spread[i - dy * NODES]
    cols = np.zeros((128, LANES))
    take = np.zeros((256, LANES))
    give = np.zeros((LANES, 2 * NODES))
    for u in range(3):
        for lane in range(128):
            comp, j = lane // 64, lane % 64 * 3 + u - SWEEPS
            dx = j // NODES
            at = u * 128 + lane
            for piece in range(3):
                first = piece * 32 + (dx + 1) * 8 + comp * PER
                cols[first : first + PER, at] = spread[j - dx * NODES]
            take[j if dx == 0 else 128 + j % NODES, at] = 1.0
            if dx == 0:
                give[at, comp * NODES + j] = 1.0
    return tuple(
        t.astype(jnp.bfloat16)
        for t in (
            left,
            twice(right, 0),
            twice(right_pair, 0),
            twice(back_right, 0),
            twice(back_left, 1),
            take,
            cols,
            rows,
            give,
        )
    )


def mm(a, b):
    return jnp.dot(a, b, preferred_element_type=f32)


def halves(value):
    hi = value.astype(bf16)
    return hi, (value - hi.astype(f32)).astype(bf16)


def iota(shape, dim):
    return lax.broadcasted_iota(jnp.int32, shape, dim)


def stacked_rows(wide):
    return jnp.concatenate([wide[:, q * PATCH : (q + 1) * PATCH] for q in range(wide.shape[1] // PATCH)], axis=0)


def side_by_side(tall):
    return jnp.concatenate([tall[q * PATCH : (q + 1) * PATCH] for q in range(tall.shape[0] // PATCH)], axis=1)


def row_pass(pixels, left):
    both = mm(left[...], pixels)
    return jnp.concatenate(halves(stacked_rows(both[:PATCH] + both[PATCH:])), axis=1)


def packed_spectrum(pixels, left, right):
    both = mm(row_pass(pixels, left), right[...])
    return both[:, :PATCH] + both[:, PATCH:]


def paired_spectrum(pixels, left, right_pair):
    both = mm(row_pass(pixels, left), right_pair[...])
    return (
        both[:, :PATCH] + both[:, 2 * PATCH : 3 * PATCH],
        both[:, PATCH : 2 * PATCH] + both[:, 3 * PATCH :],
    )


def cross_spectrum(pair, later):
    half = PATCH // 2
    same, cross = pair
    turned = pltpu.roll(later, half, 1)
    first = iota((half, PATCH), 0) == 0
    out = []
    for q in range(Q):
        top = slice(q * PATCH, q * PATCH + half)
        low = slice(q * PATCH + half, (q + 1) * PATCH)
        joint = lambda e, c: same[e] * later[c] + cross[e] * turned[c]
        low_low = joint(low, low)
        out.append(joint(top, top) + jnp.where(first, 0.0, low_low))
        out.append(jnp.where(first, low_low, joint(top, low) - joint(low, top)))
    return jnp.concatenate(out, axis=0)


def scores(product, back_right, back_left):
    both = mm(jnp.concatenate(halves(product), axis=1), back_right[...])
    wide = side_by_side(both[:, :PATCH] + both[:, PATCH:])
    both = mm(back_left[...], jnp.concatenate(halves(wide), axis=0))
    return both[:PATCH] + both[PATCH:]


def signed_lag(shape, dim):
    lag = iota(shape, dim)
    return jnp.where(lag < PATCH // 2, lag, lag - PATCH).astype(f32)


def hat(offset):
    return jnp.maximum(0.0, 1.0 - jnp.abs(offset))


def thirds(value):
    high = value.astype(bf16)
    rest = value - high.astype(f32)
    middle = rest.astype(bf16)
    return high, middle, (rest - middle.astype(f32)).astype(bf16)


def moved(value, selection):
    count = value.shape[0]
    parts = mm(jnp.concatenate(thirds(value), axis=0), selection)
    return parts[:count] + parts[count : 2 * count] + parts[2 * count :]


def kernel(
    sizes,
    images, boundary, anchor, *rest,
):
    n_gz, n_ty, n_tx = sizes
    tables_in, rest = rest[:9], rest[9:]
    (
        mesh_out, drift_out,
        own, before, after, spectra, ties, patch_in, patch_out, sums, land_in, land_out,
        rate, pull, mesh_a, mesh_b,
    ) = rest[:16]
    tables_here, rest = rest[16:25], rest[25:]
    (
        table_sem, own_sem, before_sem, after_sem, up_sem, down_sem, tie_sem, tie_sent,
        patch_sem, patch_sent, land_sem, land_sent, rounds,
    ) = rest
    left, right, right_pair, back_right, back_left, take, spread_cols, spread_rows, give = tables_here
    g, y, x = lax.axis_index("gz"), lax.axis_index("ty"), lax.axis_index("tx")

    def inside(dy, dx):
        ok = None
        for pos, step, count in ((y, dy, n_ty), (x, dx, n_tx)):
            if step:
                here = (pos + step >= 0) & (pos + step < count)
                ok = here if ok is None else ok & here
        return (g >= 0) if ok is None else ok

    def told(semaphore, ok, device):
        @pl.when(ok)
        def _():
            pl.semaphore_signal(semaphore, inc=1, device_id=device, device_id_type=MESH)

        return jnp.where(ok, 1, 0).astype(jnp.int32)

    def within(step):
        return (g + step >= 0) & (g + step < n_gz)

    near = [(within(dz), (g + dz, y, x)) for dz in (-1, 1)]
    near += [(inside(dy, dx), (g, y + dy, x + dx)) for dy, dx in SIDES]

    barrier = pltpu.get_barrier_semaphore()
    greeted = jnp.int32(0)
    for ok, device in near:
        greeted += told(barrier, ok, device)

    def band(ref, k):
        rows = pl.ds(pl.multiple_of(k // (PER // Q) * PATCH, PATCH), PATCH)
        return ref.at[rows, pl.ds(pl.multiple_of(k % (PER // Q) * WIDTH, WIDTH), WIDTH)]

    table_copies = [
        pltpu.make_async_copy(src, dst, table_sem.at[i])
        for i, (src, dst) in enumerate(zip(tables_in, tables_here))
    ]
    for copy in table_copies[:2]:
        copy.start()
    for r in range(PIECES):
        pltpu.make_async_copy(band(images.at[0], r), own.at[r], own_sem.at[r]).start()
    for copy in table_copies[2:]:
        copy.start()
    tie_own = pltpu.make_async_copy(
        anchor.at[0], ties.at[1, pl.ds(SWEEPS, NODES), :], tie_sem.at[slot(0, 0)]
    )
    tie_own.start()
    for r in range(PIECES):

        @pl.when(g == 0)
        def _():
            pltpu.make_async_copy(band(boundary, r), before.at[r], before_sem.at[r]).start()

        @pl.when(g == n_gz - 1)
        def _():
            pltpu.make_async_copy(band(boundary, r), after.at[r], after_sem.at[r]).start()

    pl.semaphore_wait(barrier, greeted)

    def remote(src, dst, sent, arrived, device):
        return pltpu.make_async_remote_copy(
            src_ref=src, dst_ref=dst, send_sem=sent, recv_sem=arrived, device_id=device, device_id_type=MESH
        )

    def to_later(r):
        return remote(own.at[r], before.at[r], up_sem.at[r], before_sem.at[r], (g + 1, y, x))

    def to_earlier(r):
        return remote(own.at[r], after.at[r], down_sem.at[r], after_sem.at[r], (g - 1, y, x))

    for r in range(PIECES):
        pltpu.make_async_copy(own.at[r], own.at[r], own_sem.at[r]).wait()

        @pl.when(g < n_gz - 1)
        def _():
            to_later(r).start()

        @pl.when(g > 0)
        def _():
            to_earlier(r).start()

    rows_of = {-1: (0, SWEEPS), 0: (0, NODES), 1: (NODES - SWEEPS, SWEEPS)}
    place_of = {-1: 0, 0: SWEEPS, 1: SWEEPS + NODES}

    def tie_copy(dy, dx):
        first, count = rows_of[dy]
        to = slot(-dy, -dx)
        return remote(
            anchor.at[0, pl.ds(first, count), :],
            ties.at[1 - dx, pl.ds(place_of[-dy], count), :],
            tie_sent.at[to],
            tie_sem.at[to],
            (g, y + dy, x + dx),
        )

    def send_ties(steps):
        for dy, dx in steps:

            @pl.when(inside(dy, dx))
            def _():
                tie_copy(dy, dx).start()

    send_ties(SIDES)
    passed = jnp.int32(0)
    for ok, device in near:
        passed += told(rounds.at[0], ok, device)

    ramp_rows = iota((8, NODES), 1).astype(f32)
    for t in range(n_gz):

        @pl.when(t >= g)
        def _():
            land_in[t] = ramp_rows

    for edge, count, first in ((y == 0, SWEEPS, 0), (y == n_ty - 1, SWEEPS, SWEEPS + NODES)):

        @pl.when(edge)
        def _():
            for d in range(3):
                ties[d, pl.ds(first, count), :] = jnp.zeros((count, NODES), f32)

    for edge, d in ((x == 0, 0), (x == n_tx - 1, 2)):

        @pl.when(edge)
        def _():
            ties[d] = jnp.zeros((WIDE, NODES), f32)

    for dy, dx in AROUND:
        if (dy, dx) != (0, 0):

            @pl.when(jnp.logical_not(inside(dy, dx)))
            def _():
                patch_in[slot(dy, dx)] = jnp.zeros((8, NODES), f32)

        @pl.when(jnp.logical_not(inside(dy, dx)) | (g < 2))
        def _():
            patch_in[9 + slot(dy, dx)] = jnp.zeros((8, NODES), f32)

    def arrival(ref, sem):
        pltpu.make_async_copy(ref, ref, sem).wait()

    for copy in table_copies[:2]:
        copy.wait()

    def own_step(r, carry):
        spectra[r] = packed_spectrum(own[r], left, right)
        return carry

    lax.fori_loop(0, PIECES // 2, own_step, 0)
    pl.semaphore_wait(rounds.at[0], passed)
    send_ties(CORNERS)
    passed_on = jnp.int32(0)
    for step in (-2, -1, 1, 2):
        passed_on += told(rounds.at[1], within(step), (g + step, y, x))
    lax.fori_loop(PIECES // 2, PIECES, own_step, 0)
    pl.semaphore_wait(rounds.at[1], passed_on)
    told(rounds.at[2], within(-4), (g - 4, y, x))

    for copy in table_copies[2:]:
        copy.wait()

    lag_rows = signed_lag((PATCH, PATCH), 0)

    def softmax_sums(wide, k):
        parts = [wide[:, i * PATCH : (i + 1) * PATCH] for i in range(2 * Q)]
        highest = jnp.concatenate([jnp.max(score, axis=0, keepdims=True) for score in parts], axis=0)
        highest = jnp.max(highest, axis=1, keepdims=True)
        for i, score in enumerate(parts):
            pair, q = i // Q, i % Q
            weight = jnp.exp2(score - highest[i : i + 1])
            at = pl.ds((k % (PER // Q) * Q + q) * PER + k // (PER // Q), 1)
            sums[pair, 0, at, :] = jnp.sum(weight, axis=0, keepdims=True)
            sums[pair, 1, at, :] = jnp.sum(weight * lag_rows, axis=0, keepdims=True)

    def band_step(k, carry):
        arrival(before.at[k], before_sem.at[k])
        arrival(after.at[k], after_sem.at[k])
        pair = paired_spectrum(before[k], left, right_pair)
        there = packed_spectrum(after[k], left, right)
        products = [cross_spectrum(pair, spectra[k]), cross_spectrum(pair, there)]
        softmax_sums(scores(jnp.concatenate(products, axis=0), back_right, back_left), k)
        return carry

    lax.fori_loop(0, PIECES, band_step, 0)

    lag_lanes = signed_lag((PER * PER, PATCH), 1)
    col_of = iota((PER * PER, 128), 1) - iota((PER * PER, 128), 0) // PER

    def flow(pair):
        weight = sums[pair, 0]
        scale = (1.0 / STRIDE) / jnp.sum(weight, axis=1, keepdims=True)
        rows = jnp.sum(sums[pair, 1], axis=1, keepdims=True) * scale
        cols = jnp.sum(weight * lag_lanes, axis=1, keepdims=True) * scale
        return rows, cols

    def patch_tile(rows, cols):
        part = jnp.where(col_of == 0, rows, jnp.where(col_of == PER, cols, 0.0))
        part = part[:8] + part[8:]
        return part + pltpu.roll(part, 4, 0)

    nearer, farther = flow(0), flow(1)
    near_scale = jnp.where(g >= 2, 0.5, 1.0).astype(f32)
    for kind, flows in ((1, [0.5 * (b - a) for a, b in zip(nearer, farther)]), (0, [near_scale * v for v in nearer])):
        tile = patch_tile(*flows)
        for d in range(3):
            value = tile if d == 0 else pltpu.roll(tile, 8 * d, 1)
            patch_out[kind, d] = value
            if (kind, d) == (0, 1):
                patch_in[slot(0, 0)] = value

    def patch_copy(kind, dy, dx):
        to = 9 * kind + slot(-dy, -dx)
        return remote(
            patch_out.at[kind, 1 - dx], patch_in.at[to], patch_sent.at[to], patch_sem.at[to],
            (g + kind, y + dy, x + dx),
        )

    ahead = (g >= 1) & (g < n_gz - 1)
    for dy, dx in sorted(AROUND, key=lambda d: -abs(d[0]) - abs(d[1])):

        @pl.when(inside(dy, dx) & ahead)
        def _():
            patch_copy(1, dy, dx).start()

        if (dy, dx) != (0, 0):

            @pl.when(inside(dy, dx))
            def _():
                patch_copy(0, dy, dx).start()

    tie_own.wait()
    for dy, dx in AROUND:
        if (dy, dx) != (0, 0):
            first, count = rows_of[-dy]
            part = ties.at[dx + 1, pl.ds(place_of[dy], count), :]

            @pl.when(inside(dy, dx))
            def _():
                arrival(part, tie_sem.at[slot(dy, dx)])

    lane8, sub8 = iota((8, 128), 1), iota((8, 128), 0)

    def limits(pos, count):
        return jnp.where(pos == 0, 0, -SWEEPS), jnp.where(pos == count - 1, NODES, NODES + SWEEPS)

    row_first, row_last = limits(y, n_ty)
    col_first, col_last = limits(x, n_tx)
    picked = []
    for group in range(GROUPS):
        at = pl.ds(group, 8, stride=GROUPS)
        picked.append(jnp.concatenate([ties[1, at, :], jnp.where(lane8 < 64, ties[2, at, :], ties[0, at, :])], axis=1))
    tie = moved(jnp.concatenate(picked, axis=0), take[...])
    for group in range(GROUPS):
        i = sub8 * GROUPS + (group - SWEEPS)
        for u in range(3):
            j = lane8 % 64 * 3 + (u - SWEEPS)
            kept = (i >= row_first) & (i < row_last) & (j >= col_first) & (j < col_last)
            value = tie[group * 8 : (group + 1) * 8, u * 128 : (u + 1) * 128]
            held = jnp.where(kept, 1.0 / (4.0 + value), 0.0)
            rate[group, :, u * 128 : (u + 1) * 128] = held
            pull[group, :, u * 128 : (u + 1) * 128] = value * held

    @pl.when(within(4))
    def _():
        pl.semaphore_wait(rounds.at[2], 1)

    for dy, dx in AROUND:

        @pl.when(inside(dy, dx) & (g >= 2))
        def _():
            arrival(patch_in.at[9 + slot(dy, dx)], patch_sem.at[9 + slot(dy, dx)])

        if (dy, dx) != (0, 0):

            @pl.when(inside(dy, dx))
            def _():
                arrival(patch_in.at[slot(dy, dx)], patch_sem.at[slot(dy, dx)])

    bands = []
    for dy in (-1, 0, 1):
        total = None
        for dx in (-1, 0, 1):
            tile = patch_in[slot(dy, dx)] + patch_in[9 + slot(dy, dx)]
            total = tile if total is None else total + tile
        bands.append(total)
    bands.append(jnp.zeros((8, 128), f32))
    high, middle, low = (v.astype(f32) for v in thirds(jnp.concatenate(bands, axis=0)))
    patches = (high + pltpu.roll(middle, 32, 1)) + pltpu.roll(low, 64, 1)
    parts = thirds(mm(patches.astype(bf16), spread_cols[...]))
    target = mm(spread_rows[...], jnp.concatenate([*parts, jnp.zeros_like(parts[0])], axis=0))
    for group in range(GROUPS):
        value = target[group * 8 : (group + 1) * 8]
        mesh_a[group] = value
        pull[group] = pull[group] * value

    def sweep(src, dst):
        for group in range(GROUPS):
            here = src[group]
            above = pltpu.roll(src[GROUPS - 1], 1, 0) if group == 0 else src[group - 1]
            below = pltpu.roll(src[0], 7, 0) if group == GROUPS - 1 else src[group + 1]
            first, second, third = (here[:, u * 128 : (u + 1) * 128] for u in range(3))
            beside = jnp.concatenate(
                [pltpu.roll(third, 1, 1) + second, first + third, second + pltpu.roll(first, 127, 1)], axis=1
            )
            dst[group] = ((above + below) + beside) * rate[group] + pull[group]

    def some_sweeps(_, carry):
        for _ in range(TRIP // 2):
            sweep(mesh_a, mesh_b)
            sweep(mesh_b, mesh_a)
        return carry

    lax.fori_loop(0, SWEEPS // TRIP, some_sweeps, 0)

    down, across = jnp.zeros((8, 128), f32), [jnp.zeros((8, 128), f32)] * 3
    for group in range(GROUPS):
        i = sub8 * GROUPS + (group - SWEEPS)
        row_inside = (i >= 0) & (i < NODES)
        row = jnp.zeros((8, 128), f32)
        for u in range(3):
            j = lane8 % 64 * 3 + (u - SWEEPS)
            value = mesh_a[group, :, u * 128 : (u + 1) * 128]
            row += jnp.where((lane8 < 64) & (j >= 0) & (j < NODES), value, 0.0)
            across[u] += jnp.where(row_inside, value, 0.0)
        down += jnp.where(lane8 == i, jnp.sum(row, axis=1, keepdims=True), 0.0)
    across = moved(jnp.concatenate(across, axis=1), give[:, NODES:])
    sub_f, lane_f = (iota((NODES, NODES), d).astype(f32) for d in (0, 1))
    ramp = lane_f[:1]
    own_rows = [
        jnp.clip(ramp + jnp.sum(value, axis=0, keepdims=True) / NODES, 0.0, NODES - 1.0)
        for value in (down, across)
    ]
    land_out[...] = jnp.where(sub8 == 0, own_rows[0], jnp.where(sub8 == 1, own_rows[1], 0.0))

    def land_copy(step):
        return remote(
            land_out, land_in.at[g], land_sent.at[step - 1], land_sem.at[g], (g + step, y, x)
        )

    for step in range(n_gz - 1, 0, -1):

        @pl.when(g + step < n_gz)
        def _():
            land_copy(step).start()

    natural = ties
    ordered = moved(jnp.concatenate([mesh_a[group] for group in range(GROUPS)], axis=0), give[...])
    for group in range(GROUPS):
        at = pl.ds(group, 8, stride=GROUPS)
        for c in range(2):
            natural[c, at, :] = ordered[group * 8 : (group + 1) * 8, c * NODES : (c + 1) * NODES]
    for c in range(2):
        mesh_out[0, c] = natural[c, SWEEPS : SWEEPS + NODES, :]

    for r in range(PIECES):

        @pl.when(g < n_gz - 1)
        def _():
            to_later(r).wait_send()

        @pl.when(g > 0)
        def _():
            to_earlier(r).wait_send()

    for dy, dx in AROUND:
        if (dy, dx) != (0, 0):

            @pl.when(inside(dy, dx))
            def _():
                tie_copy(dy, dx).wait_send()
                patch_copy(0, dy, dx).wait_send()

        @pl.when(inside(dy, dx) & ahead)
        def _():
            patch_copy(1, dy, dx).wait_send()

    eye = sub_f == lane_f
    to_row = lambda col: jnp.sum(jnp.where(eye, col, 0.0), axis=0, keepdims=True)
    to_col = lambda row: jnp.sum(jnp.where(eye, row, 0.0), axis=1, keepdims=True)
    placed = [to_col(row) for row in own_rows]
    for t in range(n_gz - 2, -1, -1):

        @pl.when(t < g)
        def _():
            arrival(land_in.at[t], land_sem.at[t])

        for c in range(2):
            landing = land_in[t, c : c + 1, :]
            if (n_gz - 2 - t) % 2 == 0:
                placed[c] = jnp.sum(hat(landing - sub_f) * placed[c], axis=0, keepdims=True)
            else:
                placed[c] = jnp.sum(hat(to_col(landing) - lane_f) * placed[c], axis=1, keepdims=True)
    for c in range(2):
        value = to_row(placed[c]) if n_gz % 2 else placed[c]
        drift_out[0, 0, 0, c : c + 1, :] = value - ramp

    for step in range(1, n_gz):

        @pl.when(g + step < n_gz)
        def _():
            land_copy(step).wait_send()


def finish(mesh_in, drift_in, mesh_out, drift_out, sems):
    copies = [
        pltpu.make_async_copy(src, dst, sems.at[i])
        for i, (src, dst) in enumerate(((mesh_in, mesh_out), (drift_in, drift_out)))
    ]
    for copy in copies:
        copy.start()
    for copy in copies:
        copy.wait()


def solution(mesh):
    sizes = tuple(mesh.shape[name] for name in ("gz", "ty", "tx"))
    n_gz = sizes[0]
    constants = tables()
    dma = pltpu.SemaphoreType.DMA
    vmem = pl.BlockSpec(memory_space=pltpu.VMEM)
    hbm = pl.BlockSpec(memory_space=pltpu.HBM)

    def local(images, boundary, anchor):
        results = (
            jax.ShapeDtypeStruct((1, 2, NODES, NODES), f32),
            jax.ShapeDtypeStruct((1, 1, 1, 2, NODES), f32),
        )
        found = pl.pallas_call(
            functools.partial(kernel, sizes),
            out_shape=results,
            in_specs=[hbm] * (3 + len(constants)),
            out_specs=(vmem, vmem),
            scratch_shapes=[
                pltpu.VMEM((PIECES, PATCH, WIDTH), bf16),
                pltpu.VMEM((PIECES, PATCH, WIDTH), bf16),
                pltpu.VMEM((PIECES, PATCH, WIDTH), bf16),
                pltpu.VMEM((PIECES, WIDTH, PATCH), f32),
                pltpu.VMEM((3, WIDE, NODES), f32),
                pltpu.VMEM((18, 8, NODES), f32),
                pltpu.VMEM((2, 3, 8, NODES), f32),
                pltpu.VMEM((2, 2, PER * PER, PATCH), f32),
                pltpu.VMEM((n_gz, 8, NODES), f32),
                pltpu.VMEM((8, NODES), f32),
                pltpu.VMEM((GROUPS, 8, LANES), f32),
                pltpu.VMEM((GROUPS, 8, LANES), f32),
                pltpu.VMEM((GROUPS, 8, LANES), f32),
                pltpu.VMEM((GROUPS, 8, LANES), f32),
                *(pltpu.VMEM(c.shape, bf16) for c in constants),
                dma((len(constants),)),
                dma((PIECES,)),
                dma((PIECES,)),
                dma((PIECES,)),
                dma((PIECES,)),
                dma((PIECES,)),
                dma((9,)),
                dma((9,)),
                dma((18,)),
                dma((18,)),
                dma((n_gz,)),
                dma((n_gz,)),
                pltpu.SemaphoreType.REGULAR((3,)),
            ],
            compiler_params=pltpu.CompilerParams(
                collective_id=0, has_side_effects=True, vmem_limit_bytes=GRANT,
            ),
            name="align",
        )(*(pltpu.with_memory_space_constraint(v, pltpu.HBM) for v in (images, boundary, anchor, *map(jnp.asarray, constants))))
        return pl.pallas_call(
            finish,
            out_shape=results,
            in_specs=[vmem, vmem],
            out_specs=(hbm, hbm),
            scratch_shapes=[dma((2,))],
            compiler_params=pltpu.CompilerParams(vmem_limit_bytes=4 * 1024 * 1024),
            name="finish",
        )(*found)

    return jax.shard_map(
        local,
        mesh=mesh,
        in_specs=(P("gz", "ty", "tx"), P("ty", "tx"), P("gz", "ty", "tx")),
        out_specs=(P("gz", None, "ty", "tx"), P("gz", "ty", "tx", None, None)),
        check_vma=False,
    )
```

```python
import functools
import math

import jax
import jax.numpy as jnp
import numpy as np
from jax import lax
from jax.experimental import pallas as pl
from jax.experimental.pallas import tpu as pltpu
from jax.sharding import PartitionSpec as P

PATCH = 128
STRIDE = 4
SWEEPS = 32
TRIP = 32
TILE = 512
NODES = 128
PER = TILE // PATCH
Q = 4
WIDTH = Q * PATCH
PIECES = PER * PER // Q
WIDE = NODES + 2 * SWEEPS
GROUPS = WIDE // 8
LANES = 2 * WIDE

GRANT = 48 * 1024 * 1024

f32 = jnp.float32
bf16 = jnp.bfloat16
MESH = pl.DeviceIdType.MESH
AROUND = [(dy, dx) for dy in (-1, 0, 1) for dx in (-1, 0, 1)]
SIDES = [(-1, 0), (1, 0), (0, -1), (0, 1)]
CORNERS = [(-1, -1), (-1, 1), (1, -1), (1, 1)]


def slot(dy, dx):
    return (dy + 1) * 3 + dx + 1


def pieces(table, count):
    parts = []
    rest = np.asarray(table, np.float64)
    for _ in range(count):
        part = rest.astype(jnp.bfloat16)
        parts.append(part)
        rest = rest - part.astype(np.float64)
    return parts


def spread_table():
    pos = (np.arange(NODES) + 0.5) * STRIDE / PATCH - 0.5
    weights = np.maximum(0.0, 1.0 - np.abs(pos[:, None] - np.arange(PER)[None, :]))
    return weights / weights.sum(axis=1, keepdims=True)


def tables():
    half = PATCH // 2
    n = np.arange(PATCH)
    angle = lambda k: 2.0 * np.pi * (n[:, None] * k[None, :] % PATCH) / PATCH
    low, high = np.arange(half), np.arange(1, half)
    cos_low, sin_high = np.cos(angle(low)), np.sin(angle(high))
    last = np.cos(np.pi * n)[:, None]
    zero = np.zeros_like(last)
    basis = np.concatenate([cos_low, last, sin_high], axis=1)
    same = np.concatenate([cos_low, last, cos_low[:, 1:]], axis=1)
    cross = np.concatenate([zero, sin_high, zero, -sin_high], axis=1)
    weight = np.full(PATCH, 2.0 / PATCH)
    weight[[0, half]] = 1.0 / PATCH
    inverse = basis * weight[None, :]

    b_hi, b_lo = pieces(basis, 2)
    s_hi, s_lo = pieces(same, 2)
    c_hi, c_lo = pieces(cross, 2)
    r_hi, r_lo = pieces(inverse.T, 2)
    l_hi, l_lo = pieces(inverse * (math.log2(math.e) / PATCH), 2)
    left = np.concatenate([b_hi.T, b_lo.T], axis=0)
    right = np.concatenate([b_hi, b_lo], axis=1)
    right_pair = np.concatenate([s_hi, c_hi, s_lo, c_lo], axis=1)
    back_right = np.concatenate([r_hi, r_lo], axis=1)
    back_left = np.concatenate([l_hi, l_lo], axis=0)
    twice = lambda t, axis: np.concatenate([t, t], axis=axis)

    spread = spread_table()
    rows = np.zeros((WIDE, 128))
    for group in range(GROUPS):
        for sub in range(8):
            i = sub * GROUPS + group - SWEEPS
            dy = i // NODES
            for piece in range(3):
                first = piece * 32 + (dy + 1) * 8
                rows[group * 8 + sub, first : first + PER] = spread[i - dy * NODES]
    cols = np.zeros((128, LANES))
    take = np.zeros((256, LANES))
    give = np.zeros((LANES, 2 * NODES))
    for u in range(3):
        for lane in range(128):
            comp, j = lane // 64, lane % 64 * 3 + u - SWEEPS
            dx = j // NODES
            at = u * 128 + lane
            for piece in range(3):
                first = piece * 32 + (dx + 1) * 8 + comp * PER
                cols[first : first + PER, at] = spread[j - dx * NODES]
            take[j if dx == 0 else 128 + j % NODES, at] = 1.0
            if dx == 0:
                give[at, comp * NODES + j] = 1.0
    return tuple(
        t.astype(jnp.bfloat16)
        for t in (
            left,
            twice(right, 0),
            twice(right_pair, 0),
            twice(back_right, 0),
            twice(back_left, 1),
            take,
            cols,
            rows,
            give,
        )
    )


def mm(a, b):
    return jnp.dot(a, b, preferred_element_type=f32)


def halves(value):
    hi = value.astype(bf16)
    return hi, (value - hi.astype(f32)).astype(bf16)


def iota(shape, dim):
    return lax.broadcasted_iota(jnp.int32, shape, dim)


def stacked_rows(wide):
    return jnp.concatenate([wide[:, q * PATCH : (q + 1) * PATCH] for q in range(wide.shape[1] // PATCH)], axis=0)


def side_by_side(tall):
    return jnp.concatenate([tall[q * PATCH : (q + 1) * PATCH] for q in range(tall.shape[0] // PATCH)], axis=1)


def row_pass(pixels, left):
    both = mm(left[...], pixels)
    return jnp.concatenate(halves(stacked_rows(both[:PATCH] + both[PATCH:])), axis=1)


def packed_spectrum(pixels, left, right):
    both = mm(row_pass(pixels, left), right[...])
    return both[:, :PATCH] + both[:, PATCH:]


def paired_spectrum(pixels, left, right_pair):
    both = mm(row_pass(pixels, left), right_pair[...])
    return (
        both[:, :PATCH] + both[:, 2 * PATCH : 3 * PATCH],
        both[:, PATCH : 2 * PATCH] + both[:, 3 * PATCH :],
    )


def cross_spectrum(pair, later):
    half = PATCH // 2
    same, cross = pair
    turned = pltpu.roll(later, half, 1)
    first = iota((half, PATCH), 0) == 0
    out = []
    for q in range(Q):
        top = slice(q * PATCH, q * PATCH + half)
        low = slice(q * PATCH + half, (q + 1) * PATCH)
        joint = lambda e, c: same[e] * later[c] + cross[e] * turned[c]
        low_low = joint(low, low)
        out.append(joint(top, top) + jnp.where(first, 0.0, low_low))
        out.append(jnp.where(first, low_low, joint(top, low) - joint(low, top)))
    return jnp.concatenate(out, axis=0)


def scores(product, back_right, back_left):
    both = mm(jnp.concatenate(halves(product), axis=1), back_right[...])
    wide = side_by_side(both[:, :PATCH] + both[:, PATCH:])
    both = mm(back_left[...], jnp.concatenate(halves(wide), axis=0))
    return both[:PATCH] + both[PATCH:]


def signed_lag(shape, dim):
    lag = iota(shape, dim)
    return jnp.where(lag < PATCH // 2, lag, lag - PATCH).astype(f32)


def hat(offset):
    return jnp.maximum(0.0, 1.0 - jnp.abs(offset))


def thirds(value):
    high = value.astype(bf16)
    rest = value - high.astype(f32)
    middle = rest.astype(bf16)
    return high, middle, (rest - middle.astype(f32)).astype(bf16)


def moved(value, selection):
    count = value.shape[0]
    parts = mm(jnp.concatenate(thirds(value), axis=0), selection)
    return parts[:count] + parts[count : 2 * count] + parts[2 * count :]


def kernel(
    sizes,
    images, boundary, anchor, *rest,
):
    n_gz, n_ty, n_tx = sizes
    tables_in, rest = rest[:9], rest[9:]
    (
        mesh_out, drift_out,
        own, before, after, spectra, ties, patch_in, patch_out, sums, land_in, land_out,
        rate, pull, mesh_a, mesh_b,
    ) = rest[:16]
    tables_here, rest = rest[16:25], rest[25:]
    (
        table_sem, own_sem, before_sem, after_sem, up_sem, down_sem, tie_sem, tie_sent,
        patch_sem, patch_sent, land_sem, land_sent, rounds,
    ) = rest
    left, right, right_pair, back_right, back_left, take, spread_cols, spread_rows, give = tables_here
    g, y, x = lax.axis_index("gz"), lax.axis_index("ty"), lax.axis_index("tx")

    def inside(dy, dx):
        ok = None
        for pos, step, count in ((y, dy, n_ty), (x, dx, n_tx)):
            if step:
                here = (pos + step >= 0) & (pos + step < count)
                ok = here if ok is None else ok & here
        return (g >= 0) if ok is None else ok

    def told(semaphore, ok, device):
        @pl.when(ok)
        def _():
            pl.semaphore_signal(semaphore, inc=1, device_id=device, device_id_type=MESH)

        return jnp.where(ok, 1, 0).astype(jnp.int32)

    def within(step):
        return (g + step >= 0) & (g + step < n_gz)

    near = [(within(dz), (g + dz, y, x)) for dz in (-1, 1)]
    near += [(inside(dy, dx), (g, y + dy, x + dx)) for dy, dx in SIDES]

    barrier = pltpu.get_barrier_semaphore()
    greeted = jnp.int32(0)
    for ok, device in near:
        greeted += told(barrier, ok, device)

    def band(ref, k):
        rows = pl.ds(pl.multiple_of(k // (PER // Q) * PATCH, PATCH), PATCH)
        return ref.at[rows, pl.ds(pl.multiple_of(k % (PER // Q) * WIDTH, WIDTH), WIDTH)]

    table_copies = [
        pltpu.make_async_copy(src, dst, table_sem.at[i])
        for i, (src, dst) in enumerate(zip(tables_in, tables_here))
    ]
    for copy in table_copies[:2]:
        copy.start()
    for r in range(PIECES):
        pltpu.make_async_copy(band(images.at[0], r), own.at[r], own_sem.at[r]).start()
    for copy in table_copies[2:]:
        copy.start()
    tie_own = pltpu.make_async_copy(
        anchor.at[0], ties.at[1, pl.ds(SWEEPS, NODES), :], tie_sem.at[slot(0, 0)]
    )
    tie_own.start()
    for r in range(PIECES):

        @pl.when(g == 0)
        def _():
            pltpu.make_async_copy(band(boundary, r), before.at[r], before_sem.at[r]).start()

        @pl.when(g == n_gz - 1)
        def _():
            pltpu.make_async_copy(band(boundary, r), after.at[r], after_sem.at[r]).start()

    pl.semaphore_wait(barrier, greeted)

    def remote(src, dst, sent, arrived, device):
        return pltpu.make_async_remote_copy(
            src_ref=src, dst_ref=dst, send_sem=sent, recv_sem=arrived, device_id=device, device_id_type=MESH
        )

    def to_later(r):
        return remote(own.at[r], before.at[r], up_sem.at[r], before_sem.at[r], (g + 1, y, x))

    def to_earlier(r):
        return remote(own.at[r], after.at[r], down_sem.at[r], after_sem.at[r], (g - 1, y, x))

    for r in range(PIECES):
        pltpu.make_async_copy(own.at[r], own.at[r], own_sem.at[r]).wait()

        @pl.when((g % 2 == 1) & (g < n_gz - 1))
        def _():
            to_later(r).start()

        @pl.when((g % 2 == 0) & (g > 0))
        def _():
            to_earlier(r).start()

    for r in range(PIECES):

        @pl.when((g % 2 == 0) & (g < n_gz - 1))
        def _():
            to_later(r).start()

        @pl.when(g % 2 == 1)
        def _():
            to_earlier(r).start()

    rows_of = {-1: (0, SWEEPS), 0: (0, NODES), 1: (NODES - SWEEPS, SWEEPS)}
    place_of = {-1: 0, 0: SWEEPS, 1: SWEEPS + NODES}

    def tie_copy(dy, dx):
        first, count = rows_of[dy]
        to = slot(-dy, -dx)
        return remote(
            anchor.at[0, pl.ds(first, count), :],
            ties.at[1 - dx, pl.ds(place_of[-dy], count), :],
            tie_sent.at[to],
            tie_sem.at[to],
            (g, y + dy, x + dx),
        )

    def send_ties(steps):
        for dy, dx in steps:

            @pl.when(inside(dy, dx))
            def _():
                tie_copy(dy, dx).start()

    send_ties(SIDES)
    passed = jnp.int32(0)
    for ok, device in near:
        passed += told(rounds.at[0], ok, device)

    ramp_rows = iota((8, NODES), 1).astype(f32)
    for t in range(n_gz):

        @pl.when(t >= g)
        def _():
            land_in[t] = ramp_rows

    for edge, count, first in ((y == 0, SWEEPS, 0), (y == n_ty - 1, SWEEPS, SWEEPS + NODES)):

        @pl.when(edge)
        def _():
            for d in range(3):
                ties[d, pl.ds(first, count), :] = jnp.zeros((count, NODES), f32)

    for edge, d in ((x == 0, 0), (x == n_tx - 1, 2)):

        @pl.when(edge)
        def _():
            ties[d] = jnp.zeros((WIDE, NODES), f32)

    for dy, dx in AROUND:
        if (dy, dx) != (0, 0):

            @pl.when(jnp.logical_not(inside(dy, dx)))
            def _():
                patch_in[slot(dy, dx)] = jnp.zeros((8, NODES), f32)

        @pl.when(jnp.logical_not(inside(dy, dx)) | (g < 2))
        def _():
            patch_in[9 + slot(dy, dx)] = jnp.zeros((8, NODES), f32)

    def arrival(ref, sem):
        pltpu.make_async_copy(ref, ref, sem).wait()

    for copy in table_copies[:2]:
        copy.wait()

    def own_step(r, carry):
        spectra[r] = packed_spectrum(own[r], left, right)
        return carry

    lax.fori_loop(0, PIECES // 2, own_step, 0)
    pl.semaphore_wait(rounds.at[0], passed)
    send_ties(CORNERS)
    passed_on = jnp.int32(0)
    for step in (-2, -1, 1, 2):
        passed_on += told(rounds.at[1], within(step), (g + step, y, x))
    lax.fori_loop(PIECES // 2, PIECES, own_step, 0)
    pl.semaphore_wait(rounds.at[1], passed_on)
    told(rounds.at[2], within(-4), (g - 4, y, x))

    for copy in table_copies[2:]:
        copy.wait()

    lag_rows = signed_lag((PATCH, PATCH), 0)

    def softmax_sums(wide, k):
        parts = [wide[:, i * PATCH : (i + 1) * PATCH] for i in range(2 * Q)]
        highest = jnp.concatenate([jnp.max(score, axis=0, keepdims=True) for score in parts], axis=0)
        highest = jnp.max(highest, axis=1, keepdims=True)
        for i, score in enumerate(parts):
            pair, q = i // Q, i % Q
            weight = jnp.exp2(score - highest[i : i + 1])
            at = pl.ds((k % (PER // Q) * Q + q) * PER + k // (PER // Q), 1)
            sums[pair, 0, at, :] = jnp.sum(weight, axis=0, keepdims=True)
            sums[pair, 1, at, :] = jnp.sum(weight * lag_rows, axis=0, keepdims=True)

    def band_step(k, carry):
        arrival(before.at[k], before_sem.at[k])
        arrival(after.at[k], after_sem.at[k])
        pair = paired_spectrum(before[k], left, right_pair)
        there = packed_spectrum(after[k], left, right)
        products = [cross_spectrum(pair, spectra[k]), cross_spectrum(pair, there)]
        softmax_sums(scores(jnp.concatenate(products, axis=0), back_right, back_left), k)
        return carry

    lax.fori_loop(0, PIECES, band_step, 0)

    lag_lanes = signed_lag((PER * PER, PATCH), 1)
    col_of = iota((PER * PER, 128), 1) - iota((PER * PER, 128), 0) // PER

    def flow(pair):
        weight = sums[pair, 0]
        scale = (1.0 / STRIDE) / jnp.sum(weight, axis=1, keepdims=True)
        rows = jnp.sum(sums[pair, 1], axis=1, keepdims=True) * scale
        cols = jnp.sum(weight * lag_lanes, axis=1, keepdims=True) * scale
        return rows, cols

    def patch_tile(rows, cols):
        part = jnp.where(col_of == 0, rows, jnp.where(col_of == PER, cols, 0.0))
        part = part[:8] + part[8:]
        return part + pltpu.roll(part, 4, 0)

    nearer, farther = flow(0), flow(1)
    near_scale = jnp.where(g >= 2, 0.5, 1.0).astype(f32)
    for kind, flows in ((1, [0.5 * (b - a) for a, b in zip(nearer, farther)]), (0, [near_scale * v for v in nearer])):
        tile = patch_tile(*flows)
        for d in range(3):
            value = tile if d == 0 else pltpu.roll(tile, 8 * d, 1)
            patch_out[kind, d] = value
            if (kind, d) == (0, 1):
                patch_in[slot(0, 0)] = value

    def patch_copy(kind, dy, dx):
        to = 9 * kind + slot(-dy, -dx)
        return remote(
            patch_out.at[kind, 1 - dx], patch_in.at[to], patch_sent.at[to], patch_sem.at[to],
            (g + kind, y + dy, x + dx),
        )

    ahead = (g >= 1) & (g < n_gz - 1)
    for dy, dx in sorted(AROUND, key=lambda d: -abs(d[0]) - abs(d[1])):

        @pl.when(inside(dy, dx) & ahead)
        def _():
            patch_copy(1, dy, dx).start()

        if (dy, dx) != (0, 0):

            @pl.when(inside(dy, dx))
            def _():
                patch_copy(0, dy, dx).start()

    tie_own.wait()
    for dy, dx in AROUND:
        if (dy, dx) != (0, 0):
            first, count = rows_of[-dy]
            part = ties.at[dx + 1, pl.ds(place_of[dy], count), :]

            @pl.when(inside(dy, dx))
            def _():
                arrival(part, tie_sem.at[slot(dy, dx)])

    lane8, sub8 = iota((8, 128), 1), iota((8, 128), 0)

    def limits(pos, count):
        return jnp.where(pos == 0, 0, -SWEEPS), jnp.where(pos == count - 1, NODES, NODES + SWEEPS)

    row_first, row_last = limits(y, n_ty)
    col_first, col_last = limits(x, n_tx)
    picked = []
    for group in range(GROUPS):
        at = pl.ds(group, 8, stride=GROUPS)
        picked.append(jnp.concatenate([ties[1, at, :], jnp.where(lane8 < 64, ties[2, at, :], ties[0, at, :])], axis=1))
    tie = moved(jnp.concatenate(picked, axis=0), take[...])
    for group in range(GROUPS):
        i = sub8 * GROUPS + (group - SWEEPS)
        for u in range(3):
            j = lane8 % 64 * 3 + (u - SWEEPS)
            kept = (i >= row_first) & (i < row_last) & (j >= col_first) & (j < col_last)
            value = tie[group * 8 : (group + 1) * 8, u * 128 : (u + 1) * 128]
            held = jnp.where(kept, 1.0 / (4.0 + value), 0.0)
            rate[group, :, u * 128 : (u + 1) * 128] = held
            pull[group, :, u * 128 : (u + 1) * 128] = value * held

    @pl.when(within(4))
    def _():
        pl.semaphore_wait(rounds.at[2], 1)

    for dy, dx in AROUND:

        @pl.when(inside(dy, dx) & (g >= 2))
        def _():
            arrival(patch_in.at[9 + slot(dy, dx)], patch_sem.at[9 + slot(dy, dx)])

        if (dy, dx) != (0, 0):

            @pl.when(inside(dy, dx))
            def _():
                arrival(patch_in.at[slot(dy, dx)], patch_sem.at[slot(dy, dx)])

    bands = []
    for dy in (-1, 0, 1):
        total = None
        for dx in (-1, 0, 1):
            tile = patch_in[slot(dy, dx)] + patch_in[9 + slot(dy, dx)]
            total = tile if total is None else total + tile
        bands.append(total)
    bands.append(jnp.zeros((8, 128), f32))
    high, middle, low = (v.astype(f32) for v in thirds(jnp.concatenate(bands, axis=0)))
    patches = (high + pltpu.roll(middle, 32, 1)) + pltpu.roll(low, 64, 1)
    parts = thirds(mm(patches.astype(bf16), spread_cols[...]))
    target = mm(spread_rows[...], jnp.concatenate([*parts, jnp.zeros_like(parts[0])], axis=0))
    for group in range(GROUPS):
        value = target[group * 8 : (group + 1) * 8]
        mesh_a[group] = value
        pull[group] = pull[group] * value

    def sweep(src, dst):
        for group in range(GROUPS):
            here = src[group]
            above = pltpu.roll(src[GROUPS - 1], 1, 0) if group == 0 else src[group - 1]
            below = pltpu.roll(src[0], 7, 0) if group == GROUPS - 1 else src[group + 1]
            first, second, third = (here[:, u * 128 : (u + 1) * 128] for u in range(3))
            beside = jnp.concatenate(
                [pltpu.roll(third, 1, 1) + second, first + third, second + pltpu.roll(first, 127, 1)], axis=1
            )
            dst[group] = ((above + below) + beside) * rate[group] + pull[group]

    def some_sweeps(_, carry):
        for _ in range(TRIP // 2):
            sweep(mesh_a, mesh_b)
            sweep(mesh_b, mesh_a)
        return carry

    lax.fori_loop(0, SWEEPS // TRIP, some_sweeps, 0)

    down, across = jnp.zeros((8, 128), f32), [jnp.zeros((8, 128), f32)] * 3
    for group in range(GROUPS):
        i = sub8 * GROUPS + (group - SWEEPS)
        row_inside = (i >= 0) & (i < NODES)
        row = jnp.zeros((8, 128), f32)
        for u in range(3):
            j = lane8 % 64 * 3 + (u - SWEEPS)
            value = mesh_a[group, :, u * 128 : (u + 1) * 128]
            row += jnp.where((lane8 < 64) & (j >= 0) & (j < NODES), value, 0.0)
            across[u] += jnp.where(row_inside, value, 0.0)
        down += jnp.where(lane8 == i, jnp.sum(row, axis=1, keepdims=True), 0.0)
    across = moved(jnp.concatenate(across, axis=1), give[:, NODES:])
    sub_f, lane_f = (iota((NODES, NODES), d).astype(f32) for d in (0, 1))
    ramp = lane_f[:1]
    own_rows = [
        jnp.clip(ramp + jnp.sum(value, axis=0, keepdims=True) / NODES, 0.0, NODES - 1.0)
        for value in (down, across)
    ]
    land_out[...] = jnp.where(sub8 == 0, own_rows[0], jnp.where(sub8 == 1, own_rows[1], 0.0))

    def land_copy(step):
        return remote(
            land_out, land_in.at[g], land_sent.at[step - 1], land_sem.at[g], (g + step, y, x)
        )

    for step in range(n_gz - 1, 0, -1):

        @pl.when(g + step < n_gz)
        def _():
            land_copy(step).start()

    natural = ties
    ordered = moved(jnp.concatenate([mesh_a[group] for group in range(GROUPS)], axis=0), give[...])
    for group in range(GROUPS):
        at = pl.ds(group, 8, stride=GROUPS)
        for c in range(2):
            natural[c, at, :] = ordered[group * 8 : (group + 1) * 8, c * NODES : (c + 1) * NODES]
    for c in range(2):
        mesh_out[0, c] = natural[c, SWEEPS : SWEEPS + NODES, :]

    for r in range(PIECES):

        @pl.when(g < n_gz - 1)
        def _():
            to_later(r).wait_send()

        @pl.when(g > 0)
        def _():
            to_earlier(r).wait_send()

    for dy, dx in AROUND:
        if (dy, dx) != (0, 0):

            @pl.when(inside(dy, dx))
            def _():
                tie_copy(dy, dx).wait_send()
                patch_copy(0, dy, dx).wait_send()

        @pl.when(inside(dy, dx) & ahead)
        def _():
            patch_copy(1, dy, dx).wait_send()

    eye = sub_f == lane_f
    to_row = lambda col: jnp.sum(jnp.where(eye, col, 0.0), axis=0, keepdims=True)
    to_col = lambda row: jnp.sum(jnp.where(eye, row, 0.0), axis=1, keepdims=True)
    placed = [to_col(row) for row in own_rows]
    for t in range(n_gz - 2, -1, -1):

        @pl.when(t < g)
        def _():
            arrival(land_in.at[t], land_sem.at[t])

        for c in range(2):
            landing = land_in[t, c : c + 1, :]
            if (n_gz - 2 - t) % 2 == 0:
                placed[c] = jnp.sum(hat(landing - sub_f) * placed[c], axis=0, keepdims=True)
            else:
                placed[c] = jnp.sum(hat(to_col(landing) - lane_f) * placed[c], axis=1, keepdims=True)
    for c in range(2):
        value = to_row(placed[c]) if n_gz % 2 else placed[c]
        drift_out[0, 0, 0, c : c + 1, :] = value - ramp

    for step in range(1, n_gz):

        @pl.when(g + step < n_gz)
        def _():
            land_copy(step).wait_send()


def finish(mesh_in, drift_in, mesh_out, drift_out, sems):
    copies = [
        pltpu.make_async_copy(src, dst, sems.at[i])
        for i, (src, dst) in enumerate(((mesh_in, mesh_out), (drift_in, drift_out)))
    ]
    for copy in copies:
        copy.start()
    for copy in copies:
        copy.wait()


def solution(mesh):
    sizes = tuple(mesh.shape[name] for name in ("gz", "ty", "tx"))
    n_gz = sizes[0]
    constants = tables()
    dma = pltpu.SemaphoreType.DMA
    vmem = pl.BlockSpec(memory_space=pltpu.VMEM)
    hbm = pl.BlockSpec(memory_space=pltpu.HBM)

    def local(images, boundary, anchor):
        results = (
            jax.ShapeDtypeStruct((1, 2, NODES, NODES), f32),
            jax.ShapeDtypeStruct((1, 1, 1, 2, NODES), f32),
        )
        found = pl.pallas_call(
            functools.partial(kernel, sizes),
            out_shape=results,
            in_specs=[hbm] * (3 + len(constants)),
            out_specs=(vmem, vmem),
            scratch_shapes=[
                pltpu.VMEM((PIECES, PATCH, WIDTH), bf16),
                pltpu.VMEM((PIECES, PATCH, WIDTH), bf16),
                pltpu.VMEM((PIECES, PATCH, WIDTH), bf16),
                pltpu.VMEM((PIECES, WIDTH, PATCH), f32),
                pltpu.VMEM((3, WIDE, NODES), f32),
                pltpu.VMEM((18, 8, NODES), f32),
                pltpu.VMEM((2, 3, 8, NODES), f32),
                pltpu.VMEM((2, 2, PER * PER, PATCH), f32),
                pltpu.VMEM((n_gz, 8, NODES), f32),
                pltpu.VMEM((8, NODES), f32),
                pltpu.VMEM((GROUPS, 8, LANES), f32),
                pltpu.VMEM((GROUPS, 8, LANES), f32),
                pltpu.VMEM((GROUPS, 8, LANES), f32),
                pltpu.VMEM((GROUPS, 8, LANES), f32),
                *(pltpu.VMEM(c.shape, bf16) for c in constants),
                dma((len(constants),)),
                dma((PIECES,)),
                dma((PIECES,)),
                dma((PIECES,)),
                dma((PIECES,)),
                dma((PIECES,)),
                dma((9,)),
                dma((9,)),
                dma((18,)),
                dma((18,)),
                dma((n_gz,)),
                dma((n_gz,)),
                pltpu.SemaphoreType.REGULAR((3,)),
            ],
            compiler_params=pltpu.CompilerParams(
                collective_id=0, has_side_effects=True, vmem_limit_bytes=GRANT,
            ),
            name="align",
        )(*(pltpu.with_memory_space_constraint(v, pltpu.HBM) for v in (images, boundary, anchor, *map(jnp.asarray, constants))))
        return pl.pallas_call(
            finish,
            out_shape=results,
            in_specs=[vmem, vmem],
            out_specs=(hbm, hbm),
            scratch_shapes=[dma((2,))],
            compiler_params=pltpu.CompilerParams(vmem_limit_bytes=4 * 1024 * 1024),
            name="finish",
        )(*found)

    return jax.shard_map(
        local,
        mesh=mesh,
        in_specs=(P("gz", "ty", "tx"), P("ty", "tx"), P("gz", "ty", "tx")),
        out_specs=(P("gz", None, "ty", "tx"), P("gz", "ty", "tx", None, None)),
        check_vma=False,
    )
```
